128 devices in a mesh: group: 16 (over y, x), hidden: 8 (over z, core).
Axes of the slice: x: 4, y: 4, z: 4, core: 2. Of those that a mesh axis runs over, the one named last changes fastest.
Arguments:
- queries: bfloat16 [6144, 4096], P('group', 'hidden'), may hold values from -16 to 16, as said below
- key_rows: bfloat16 [6144, 512], P('group'), may hold values from -16 to 16
- value_rows: bfloat16 [6144, 512], P('group'), may hold values from -6 to 6
- out_proj: bfloat16 [4096, 2048], P('hidden'), may hold values from -0.09375 to 0.09375
- residual: bfloat16 [6144, 2048], P('group'), may hold values from -120 to 120
- norm_gain: float32 [2048], replicated, may hold values from 0.1 to 1.9
- w_gate: bfloat16 [128, 2048, 768], P('group', None, 'hidden'), may hold values from -0.125 to 0.125
- w_up: bfloat16 [128, 2048, 768], P('group', None, 'hidden'), may hold values from -0.125 to 0.125
- w_down: bfloat16 [128, 768, 2048], P('group', 'hidden'), may hold values from -0.21875 to 0.21875
- route_slot: int32 [6144, 8], P('group'), may hold values from 0 to 15, all different within a row; in each aligned block of 384 rows (0 to 383, 384 to 767, ...) at most 240 rows name the same one
- route_weight: float32 [6144, 8], P('group'), may hold values from 0.05 to 0.3
- fetch_list: int32 [16, 16], replicated, may hold values from 0 to 127, as said below
- cotangent: bfloat16 [6144, 2048], P('group'), may hold values from -6 to 6
Outputs:
- layer_out: bfloat16 [6144, 2048], P('group', 'hidden')
- grad_normed: bfloat16 [6144, 2048], P('group', 'hidden')
- grad_gate: bfloat16 [128, 2048, 768], P('group', None, 'hidden')
- grad_up: bfloat16 [128, 2048, 768], P('group', None, 'hidden')
- grad_down: bfloat16 [128, 768, 2048], P('group', 'hidden')
The draws below stay inside these ranges and needn't reach their ends.
Inputs may be any that keep to these rules, and one draw needn't show every extreme that they name: `queries`: queries and keys lie within the range. `route_slot`: within each group's 384 tokens no entry is named by more than 240 tokens, a bound that some block reaches; a token's 8 entries differ. `fetch_list`: entry f of every group's list is an expert owned by owner group f, that is an id from (f) * 8 to (f) * 8 + 7; the ids of one group's list differ.
All inputs are finite; a program needn't handle non-finite values.
Results may differ from the reference program's by a relative error of at most 0.017.
Values may be sent and summed in bfloat16 or wider, within the bound.
No kernel may reach another device: no remote copies, remote signals or barrier semaphores. Data moves between devices by JAX's collectives and lax.ppermute only.
A program may use at most 256 MiB of HBM per device.

```python
import math
import jax
import jax.numpy as jnp
import numpy as np
from jax import lax

D = 2048
FF = 768
HEADS = 32
KV_HEADS = 4
HEAD_DIM = 128
TOPK = 8
EXP_GROUP = 8
FETCH = 16
TOK_GROUP = 384
CAP = 240
EXPERTS = 128
TOKENS = 6144
N_GROUP = 16
N_HIDDEN = 8


def pair_draws(key):
    key_keys, key_queries = jax.random.split(jax.random.fold_in(key, 7), 2)
    keys_out = jnp.clip(jax.random.normal(key_keys, (TOKENS, KV_HEADS * HEAD_DIM), jnp.float32), -4.0, 4.0)
    queries_out = jnp.clip(jax.random.normal(key_queries, (TOKENS, HEADS * HEAD_DIM), jnp.float32), -4.0, 4.0)
    return (keys_out, queries_out)


def draw_queries(key, part):
    return pair_draws(key)[1].astype(jnp.bfloat16)


def draw_key_rows(key, part):
    return pair_draws(key)[0].astype(jnp.bfloat16)


def draw_residual(key, part):
    key_values = jax.random.fold_in(jax.random.fold_in(key, 3), 0)
    values = jnp.clip(jax.random.normal(key_values, (TOKENS, D), jnp.float32), -4.0, 4.0)
    return values.astype(jnp.bfloat16)


def draw_fetch_list(key, part):
    per_owner = FETCH // N_GROUP
    scores = jax.random.randint(jax.random.fold_in(key, 5), (N_GROUP, N_GROUP, EXP_GROUP), 0, 1 << 20) * EXP_GROUP
    scores = scores + jnp.arange(EXP_GROUP, dtype=jnp.int32)[None, None, :]
    order = jnp.argsort(scores, axis=-1, stable=True)[:, :, :per_owner]
    ids = order + (jnp.arange(N_GROUP, dtype=jnp.int32) * EXP_GROUP)[None, :, None]
    return ids.reshape(N_GROUP, FETCH).astype(jnp.int32)


def block_levels(key, extent, pieces, smallest, largest):
    factor_of, own = 1.0, jax.random.fold_in(key, 6)
    for dim, blocks in pieces:
        steps = jnp.exp(jax.random.uniform(jax.random.fold_in(own, dim), (blocks,), jnp.float32, smallest / len(pieces), largest / len(pieces)))
        factor_of = factor_of * jnp.repeat(steps, extent[dim] // blocks).reshape([-1 if axis == dim else 1 for axis in range(len(extent))])
    return factor_of


def deal_out(key, own, number, rows, amount, top, most, skew):
    ranking = jax.random.permutation(key, amount)
    crowded, usual = load_shares(amount, rows * top, most, skew, True), load_shares(amount, rows * top, most, skew, False)
    places = jnp.arange(amount)

    def named(sizes, offset_by):
        used = int((sizes > 0).sum())
        fixed = max(1, used // 4)
        moved = fixed + (places - fixed + offset_by * (used - fixed)) % max(1, amount - fixed)
        return jnp.zeros((amount,), jnp.int32).at[ranking[jnp.where(places < fixed, places, moved)]].set(jnp.asarray(sizes, jnp.int32))

    sizes = jnp.where(number % 4 == 0, named(crowded, number // 4), named(usual, number - number // 4 - 1))
    mixed = jax.random.permutation(jax.random.fold_in(own, 3), amount)
    giver, receiver = mixed[0:amount // 2 * 2:2], mixed[1:amount // 2 * 2:2]
    slack = jnp.minimum(sizes[giver] - 1, most - sizes[receiver]) // 2
    slack = jnp.where((giver == ranking[0]) | (receiver == ranking[0]) | (sizes[receiver] == 0), 0, jnp.maximum(slack, 0))
    moved = jax.random.randint(jax.random.fold_in(own, 4), (amount // 2,), 0, 1 << 20) % (slack + 1)
    sizes = sizes.at[giver].add(-moved).at[receiver].add(moved)
    items = jnp.searchsorted(jnp.cumsum(sizes), jnp.arange(rows * top), side="right").astype(jnp.int32)
    listing = items.reshape(top, rows).T
    listing = listing[jax.random.permutation(jax.random.fold_in(own, 1), rows)]
    offset_by = jax.random.randint(jax.random.fold_in(own, 2), (rows, 1), 0, top)
    return jnp.take_along_axis(listing, (jnp.arange(top)[None, :] + offset_by) % top, axis=1)


def load_shares(amount, total, bound, slope, full):
    weights = [(1 << 20) // math.isqrt(standing ** slope) + 1 for standing in range(1, amount + 1)]
    largest = bound if full else min(bound, max(-(-total // amount), total * weights[0] // sum(weights)))
    least = 1 if total - largest >= amount - 1 else 0
    counts, rest = [largest] + [least] * (amount - 1), total - largest - least * (amount - 1)
    while rest > 0:
        candidates = [i for i in range(1, amount) if counts[i] < largest] or [i for i in range(1, amount) if counts[i] < bound]
        whole, left = sum([weights[i] for i in candidates]), rest
        for i in candidates:
            addition = min(bound - counts[i], max(1, left * weights[i] // whole), rest)
            counts[i] = counts[i] + addition
            rest = rest - addition
    return np.array(counts)


def bell_draw(stream_key, dims, width, limit, pieces=(), kind=jnp.bfloat16):
    values = width * jax.random.normal(stream_key, dims, jnp.float32)
    if pieces:
        values = values * block_levels(stream_key, dims, pieces, -0.22, 0.18)
    return jnp.clip(values, -limit, limit).astype(kind)


def setup_inputs(seed: int = 0) -> dict:
    arg_keys = jax.random.split(jax.random.key(seed), 14)
    queries = draw_queries(jax.random.fold_in(arg_keys[13], 71), 0)
    key_rows = draw_key_rows(jax.random.fold_in(arg_keys[13], 71), 0)
    value_rows = bell_draw(arg_keys[2], (TOKENS, KV_HEADS * HEAD_DIM), 1.0, 6.0, ((0, 16),))
    out_proj = bell_draw(arg_keys[3], (HEADS * HEAD_DIM, D), (HEADS * HEAD_DIM) ** -0.5, 0.09375, ((0, 8),))
    residual = draw_residual(jax.random.fold_in(arg_keys[13], 71), 0)
    norm_gain = jnp.clip(1.0 + 0.18 * jax.random.normal(arg_keys[5], (D,), jnp.float32), 0.1, 1.9)
    w_gate = bell_draw(arg_keys[6], (EXPERTS, D, FF), D ** -0.5, 0.125, ((0, 16), (2, 8)))
    w_up = bell_draw(arg_keys[7], (EXPERTS, D, FF), D ** -0.5, 0.125, ((0, 16), (2, 8)))
    w_down = bell_draw(arg_keys[8], (EXPERTS, FF, D), FF ** -0.5, 0.21875, ((0, 16), (1, 8)))
    route_slot_keys = jax.random.split(jax.random.fold_in(arg_keys[9], 1), TOKENS // TOK_GROUP)
    route_slot_turns = jax.random.permutation(jax.random.fold_in(arg_keys[9], 3), TOKENS // TOK_GROUP)
    route_slot = jax.vmap(lambda own, number: deal_out(jax.random.fold_in(arg_keys[9], 2), own, number, TOK_GROUP, FETCH, TOPK, CAP, 2))(route_slot_keys, route_slot_turns).reshape((TOKENS, TOPK))
    route_weight = jnp.clip(0.05 + 0.25 * jax.random.uniform(arg_keys[10], (TOKENS, TOPK), jnp.float32) ** block_levels(arg_keys[10], (TOKENS, TOPK), ((0, 16),), -0.2, 0.2), 0.05, 0.3)
    fetch_list = draw_fetch_list(jax.random.fold_in(arg_keys[13], 71), 0)
    cotangent = bell_draw(arg_keys[12], (TOKENS, D), 1.0, 6.0, ((0, 16),))
    return dict(queries=queries, key_rows=key_rows, value_rows=value_rows, out_proj=out_proj, residual=residual, norm_gain=norm_gain, w_gate=w_gate, w_up=w_up, w_down=w_down, route_slot=route_slot, route_weight=route_weight, fetch_list=fetch_list, cotangent=cotangent)


epsilon = 1e-06

def attend(query_in, key_in, value_in):
    tokens_here = query_in.shape[0]
    query_heads = query_in.reshape(tokens_here, HEADS, HEAD_DIM).astype(jnp.float32)
    key_heads = jnp.repeat(key_in.reshape(tokens_here, KV_HEADS, HEAD_DIM).astype(jnp.float32), HEADS // KV_HEADS, axis=1)
    value_heads = jnp.repeat(value_in.reshape(tokens_here, KV_HEADS, HEAD_DIM).astype(jnp.float32), HEADS // KV_HEADS, axis=1)
    scores = jnp.einsum('thd,shd->hts', query_heads, key_heads) / math.sqrt(HEAD_DIM)
    row_pos = jnp.arange(tokens_here, dtype=jnp.int32)[:, None]
    col_pos = jnp.arange(tokens_here, dtype=jnp.int32)[None, :]
    scores = jnp.where(row_pos >= col_pos, scores, -1e+30)
    row_peak = lax.optimization_barrier(jnp.max(scores, axis=-1, keepdims=True))
    weights = jnp.exp(scores - row_peak)
    probabilities = (weights / lax.optimization_barrier(jnp.sum(weights, axis=-1, keepdims=True))).astype(jnp.bfloat16)
    mixed = jnp.einsum('hts,shd->thd', probabilities.astype(jnp.float32), value_heads)
    return mixed.astype(jnp.bfloat16).reshape(tokens_here, HEADS * HEAD_DIM)

def route_table(slots, weights, fetch_count, capacity):
    tokens_here = slots.shape[0]
    slot_ids = jnp.arange(fetch_count, dtype=jnp.int32)
    chosen = slots[:, :, None] == slot_ids[None, None, :]
    slot_weight = lax.optimization_barrier(jnp.sum(jnp.where(chosen, weights[:, :, None], 0.0), axis=1))
    is_used = jnp.any(chosen, axis=1)
    position = jnp.cumsum(is_used.astype(jnp.int32), axis=0) - 1
    target = jnp.where(is_used, slot_ids[None, :] * capacity + position, fetch_count * capacity).astype(jnp.int32)
    token_ids = jnp.broadcast_to(jnp.arange(tokens_here, dtype=jnp.int32)[:, None], (tokens_here, fetch_count))
    rows = jnp.zeros((fetch_count * capacity + 1,), jnp.int32).at[target.reshape(-1)].set(token_ids.reshape(-1))
    row_weight = jnp.zeros((fetch_count * capacity + 1,), weights.dtype).at[target.reshape(-1)].set(slot_weight.reshape(-1))
    return (rows[:-1].reshape(fetch_count, capacity), row_weight[:-1].reshape(fetch_count, capacity))

def sum_rounded(parts):
    rounded = lax.optimization_barrier(parts.astype(jnp.bfloat16))
    return lax.optimization_barrier(jnp.sum(rounded.astype(jnp.float32), axis=0))

def expert_block(routed_rows, routed_grad, row_weight, rows, gate_block, up_block, down_block):
    tokens_here = TOK_GROUP
    x_rows = routed_rows.astype(jnp.float32)
    gate_f = gate_block.astype(jnp.float32)
    up_f = up_block.astype(jnp.float32)
    down_f = down_block.astype(jnp.float32)
    pre_gate = jnp.einsum('fcd,fdh->fch', x_rows, gate_f)
    pre_up = jnp.einsum('fcd,fdh->fch', x_rows, up_f)
    sigmoid_gate = jax.nn.sigmoid(pre_gate)
    swish = pre_gate * sigmoid_gate
    activated = (swish * pre_up).astype(jnp.bfloat16)
    expert_out = jnp.einsum('fch,fhd->fcd', activated.astype(jnp.float32), down_f)
    flat_rows = rows.reshape(-1)
    out_part = jnp.zeros((tokens_here, D), jnp.float32).at[flat_rows].add((expert_out * row_weight[..., None]).reshape(-1, D))
    grad_rows = routed_grad.astype(jnp.float32)
    d_act = jnp.einsum('fcd,fhd->fch', grad_rows, down_f)
    d_gate = (d_act * pre_up * sigmoid_gate * (1.0 + pre_gate * (1.0 - sigmoid_gate))).astype(jnp.bfloat16)
    d_up = (d_act * swish).astype(jnp.bfloat16)
    grad_down_part = jnp.einsum('fch,fcd->fhd', activated.astype(jnp.float32), grad_rows).astype(jnp.bfloat16)
    grad_gate_part = jnp.einsum('fcd,fch->fdh', x_rows, d_gate.astype(jnp.float32)).astype(jnp.bfloat16)
    grad_up_part = jnp.einsum('fcd,fch->fdh', x_rows, d_up.astype(jnp.float32)).astype(jnp.bfloat16)
    d_rows = jnp.einsum('fch,fdh->fcd', d_gate.astype(jnp.float32), gate_f) + jnp.einsum('fch,fdh->fcd', d_up.astype(jnp.float32), up_f)
    input_part = jnp.zeros((tokens_here, D), jnp.float32).at[flat_rows].add(d_rows.reshape(-1, D))
    return (out_part, input_part, grad_gate_part, grad_up_part, grad_down_part)

def reference(queries, key_rows, value_rows, out_proj, residual, norm_gain, w_gate, w_up, w_down, route_slot, route_weight, fetch_list, cotangent):

    def by_group(array):
        return array.reshape((N_GROUP, TOK_GROUP) + array.shape[1:])
    head_cols = HEADS * HEAD_DIM // N_HIDDEN
    unit_block = FF // N_HIDDEN

    def one_group(carry, inputs):
        sum_gate, sum_up, sum_down = carry
        query_g, key_g, value_g, resid_g, slot_g, weight_g, cot_g, fetch_g = inputs
        mixed = attend(query_g, key_g, value_g)
        attn_parts = jnp.einsum('tnc,ncd->ntd', mixed.reshape(TOK_GROUP, N_HIDDEN, head_cols).astype(jnp.float32), out_proj.reshape(N_HIDDEN, head_cols, D).astype(jnp.float32))
        stream = resid_g.astype(jnp.float32) + sum_rounded(attn_parts)
        mean_square = lax.optimization_barrier(jnp.mean(stream * stream, axis=-1, keepdims=True))
        normed = (stream * lax.rsqrt(mean_square + epsilon) * norm_gain).astype(jnp.bfloat16)
        rows, row_weight = route_table(slot_g, weight_g, FETCH, CAP)
        routed_rows = normed[rows]
        routed_grad = (cot_g[rows].astype(jnp.float32) * row_weight[..., None]).astype(jnp.bfloat16)
        gate_sel = w_gate[fetch_g].reshape(FETCH, D, N_HIDDEN, unit_block).transpose(2, 0, 1, 3)
        up_sel = w_up[fetch_g].reshape(FETCH, D, N_HIDDEN, unit_block).transpose(2, 0, 1, 3)
        down_sel = w_down[fetch_g].reshape(FETCH, N_HIDDEN, unit_block, D).transpose(1, 0, 2, 3)

        def block_work(blocks):
            return expert_block(routed_rows, routed_grad, row_weight, rows, blocks[0], blocks[1], blocks[2])
        out_parts, input_parts, gate_parts, up_parts, down_parts = lax.map(block_work, (gate_sel, up_sel, down_sel))
        moe_out = sum_rounded(out_parts)
        grad_in = sum_rounded(input_parts)
        gate_full = gate_parts.transpose(1, 2, 0, 3).reshape(FETCH, D, FF)
        up_full = up_parts.transpose(1, 2, 0, 3).reshape(FETCH, D, FF)
        down_full = down_parts.transpose(1, 0, 2, 3).reshape(FETCH, FF, D)
        sum_gate = sum_gate.at[fetch_g].add(gate_full.astype(jnp.float32))
        sum_up = sum_up.at[fetch_g].add(up_full.astype(jnp.float32))
        sum_down = sum_down.at[fetch_g].add(down_full.astype(jnp.float32))
        outputs = ((stream + moe_out).astype(jnp.bfloat16), grad_in.astype(jnp.bfloat16))
        return ((sum_gate, sum_up, sum_down), outputs)
    start = (jnp.zeros((EXPERTS, D, FF), jnp.float32), jnp.zeros((EXPERTS, D, FF), jnp.float32), jnp.zeros((EXPERTS, FF, D), jnp.float32))
    inputs = (by_group(queries), by_group(key_rows), by_group(value_rows), by_group(residual), by_group(route_slot), by_group(route_weight), by_group(cotangent), fetch_list)
    sums, outputs = lax.scan(one_group, start, inputs)
    layer_out = outputs[0].reshape(TOKENS, D)
    grad_normed = outputs[1].reshape(TOKENS, D)
    return (layer_out, grad_normed, sums[0].astype(jnp.bfloat16), sums[1].astype(jnp.bfloat16), sums[2].astype(jnp.bfloat16))
```

```python
import math

import jax
import jax.numpy as jnp
from jax import lax
from jax.experimental import pallas as pl
from jax.experimental.pallas import tpu as pltpu
from jax.sharding import PartitionSpec as P

D = 2048
HEADS = 32
KV_HEADS = 4
HEAD_DIM = 128
EXP_GROUP = 8
FETCH = 16
CAP = 240
UNITS = 96
PAD = 128
COLS = 256
HALF = 1024
STEPS = FETCH + EXP_GROUP

epsilon = 1e-06
bf16 = jnp.bfloat16
f32 = jnp.float32

NT = (((1,), (1,)), ((), ()))
NN = (((1,), (0,)), ((), ()))
TN = (((0,), (0,)), ((), ()))


def mm(a, b, dims):
    return lax.dot_general(a, b, dims, preferred_element_type=f32)


def attention(queries, key_block, value_block):
    tokens = queries.shape[0]
    heads = queries.shape[1] // HEAD_DIM
    query = queries.reshape(tokens, heads, HEAD_DIM)
    scores = jnp.einsum("thd,sd->hts", query, key_block, preferred_element_type=f32)
    scores = scores / math.sqrt(HEAD_DIM)
    row_pos = lax.broadcasted_iota(jnp.int32, (tokens, tokens), 0)
    col_pos = lax.broadcasted_iota(jnp.int32, (tokens, tokens), 1)
    scores = jnp.where(row_pos >= col_pos, scores, -1e30)
    weights = jnp.exp(scores - jnp.max(scores, axis=-1, keepdims=True))
    probs = (weights / jnp.sum(weights, axis=-1, keepdims=True)).astype(bf16)
    mixed = jnp.einsum("hts,sd->thd", probs, value_block, preferred_element_type=f32)
    return mixed.astype(bf16).reshape(tokens, heads * HEAD_DIM)


def rows_kernel(
    expert_ref, core_ref, x_ref, g_own_ref, g_oth_ref, wg_ref, wu_ref, wd_ref,
    out_ref, d_own_ref, d_oth_ref, act_ref, dgu_ref, wgu, wdp,
):
    core = core_ref[0]

    @pl.when(pl.program_id(0) == 0)
    def _():
        zeros = jnp.zeros((PAD - UNITS, D), bf16)
        wgu[UNITS:PAD, :] = zeros
        wgu[PAD + UNITS :, :] = zeros
        wdp[UNITS:, :] = zeros

    wgu[:UNITS, :] = wg_ref[0]
    wgu[PAD : PAD + UNITS, :] = wu_ref[0]
    wdp[:UNITS, :] = wd_ref[0]

    pre = jnp.zeros((CAP, 2 * PAD), f32)
    for block in range(D // COLS):
        pre = pre + mm(x_ref[block, 0], wgu[:, block * COLS : (block + 1) * COLS], NT)
    own = pl.multiple_of(core * HALF, HALF)
    oth = pl.multiple_of(HALF - core * HALF, HALF)
    d_act = mm(g_own_ref[0], wdp[:, pl.ds(own, HALF)], NT) + mm(
        g_oth_ref[0], wdp[:, pl.ds(oth, HALF)], NT
    )
    gate, up = pre[:, :PAD], pre[:, PAD:]
    sig = jax.nn.sigmoid(gate)
    swish = gate * sig
    act = (swish * up).astype(bf16)
    d_gate = (d_act * up * sig * (1.0 + gate * (1.0 - sig))).astype(bf16)
    d_up = (d_act * swish).astype(bf16)
    act_ref[0] = act
    dgu_ref[0, :, :PAD] = d_gate
    dgu_ref[0, :, PAD:] = d_up
    for block in range(D // COLS):
        out_ref[block, 0] = mm(act, wdp[:, block * COLS : (block + 1) * COLS], NN).astype(bf16)
    d_gu = dgu_ref[0]
    for block in range(4):
        place = slice(block * COLS, (block + 1) * COLS)
        col = pl.multiple_of((2 * block + core) * COLS, COLS)
        d_own_ref[0, :, place] = mm(d_gu, wgu[:, pl.ds(col, COLS)], NN).astype(bf16)
        col = pl.multiple_of((2 * block + 1 - core) * COLS, COLS)
        d_oth_ref[0, :, place] = mm(d_gu, wgu[:, pl.ds(col, COLS)], NN).astype(bf16)


def rows_call(experts, core, x_rows, g_own, g_oth, wg, wu, wd):
    weight = pl.BlockSpec((1, UNITS, D), lambda i, e, c: (e[i], 0, 0))
    cols8 = pl.BlockSpec((8, 1, CAP, COLS), lambda i, e, c: (0, i, 0, 0))
    half = pl.BlockSpec((1, CAP, HALF), lambda i, e, c: (i, 0, 0))
    return pl.pallas_call(
        rows_kernel,
        grid_spec=pltpu.PrefetchScalarGridSpec(
            num_scalar_prefetch=2,
            grid=(FETCH,),
            in_specs=[cols8, half, half, weight, weight, weight],
            out_specs=[
                cols8,
                half,
                half,
                pl.BlockSpec((1, CAP, PAD), lambda i, e, c: (i, 0, 0)),
                pl.BlockSpec((1, CAP, 2 * PAD), lambda i, e, c: (i, 0, 0)),
            ],
            scratch_shapes=[pltpu.VMEM((2 * PAD, D), bf16), pltpu.VMEM((PAD, D), bf16)],
        ),
        out_shape=[
            jax.ShapeDtypeStruct((8, FETCH, CAP, COLS), bf16),
            jax.ShapeDtypeStruct((FETCH, CAP, HALF), bf16),
            jax.ShapeDtypeStruct((FETCH, CAP, HALF), bf16),
            jax.ShapeDtypeStruct((FETCH, CAP, PAD), bf16),
            jax.ShapeDtypeStruct((FETCH, CAP, 2 * PAD), bf16),
        ],
        compiler_params=pltpu.CompilerParams(vmem_limit_bytes=48 << 20),
        cost_estimate=pl.CostEstimate(
            flops=2 * 6 * FETCH * CAP * D * PAD, bytes_accessed=85 << 20, transcendentals=0
        ),
        name="expert_rows",
    )(experts, core, x_rows, g_own, g_oth, wg, wu, wd)


def grads_kernel(
    chunk_ref, expert_ref, real_ref, last_ref, core_ref, x_ref, g_own_ref, g_oth_ref,
    act_ref, dgu_ref, gg_ref, gu_ref, gd_ref, acc_gu, acc_d,
):
    step = pl.program_id(0)
    core = core_ref[0]

    @pl.when(real_ref[step] == 0)
    def _():
        acc_gu[...] = jnp.zeros_like(acc_gu)
        acc_d[...] = jnp.zeros_like(acc_d)

    @pl.when(real_ref[step] == 1)
    def _():
        d_gu, act = dgu_ref[0], act_ref[0]
        for block in range(D // COLS):
            place = slice(block * COLS, (block + 1) * COLS)
            acc_gu[:, place] += mm(d_gu, x_ref[block, 0], TN)
        for block in range(HALF // COLS):
            place = slice(block * COLS, (block + 1) * COLS)
            col = pl.multiple_of(core * HALF + block * COLS, COLS)
            acc_d[:, pl.ds(col, COLS)] += mm(act, g_own_ref[0, :, place], TN)
            col = pl.multiple_of(HALF - core * HALF + block * COLS, COLS)
            acc_d[:, pl.ds(col, COLS)] += mm(act, g_oth_ref[0, :, place], TN)

    @pl.when(last_ref[step] == 1)
    def _():
        gg_ref[0] = acc_gu[:UNITS, :].astype(bf16)
        gu_ref[0] = acc_gu[PAD : PAD + UNITS, :].astype(bf16)
        gd_ref[0] = acc_d[:UNITS, :].astype(bf16)


def grads_call(chunk, expert, real, last, core, x_rows, g_own, g_oth, act, dgu):
    weight = pl.BlockSpec((1, UNITS, D), lambda i, k, e, r, l, c: (e[i], 0, 0))
    half = pl.BlockSpec((1, CAP, HALF), lambda i, k, e, r, l, c: (k[i], 0, 0))
    return pl.pallas_call(
        grads_kernel,
        grid_spec=pltpu.PrefetchScalarGridSpec(
            num_scalar_prefetch=5,
            grid=(STEPS,),
            in_specs=[
                pl.BlockSpec((8, 1, CAP, COLS), lambda i, k, e, r, l, c: (0, k[i], 0, 0)),
                half,
                half,
                pl.BlockSpec((1, CAP, PAD), lambda i, k, e, r, l, c: (k[i], 0, 0)),
                pl.BlockSpec((1, CAP, 2 * PAD), lambda i, k, e, r, l, c: (k[i], 0, 0)),
            ],
            out_specs=[weight, weight, weight],
            scratch_shapes=[pltpu.VMEM((2 * PAD, D), f32), pltpu.VMEM((PAD, D), f32)],
        ),
        out_shape=[jax.ShapeDtypeStruct((EXP_GROUP, UNITS, D), bf16)] * 3,
        compiler_params=pltpu.CompilerParams(vmem_limit_bytes=48 << 20),
        cost_estimate=pl.CostEstimate(
            flops=2 * 3 * FETCH * CAP * D * PAD, bytes_accessed=45 << 20, transcendentals=0
        ),
        name="weight_grads",
    )(chunk, expert, real, last, core, x_rows, g_own, g_oth, act, dgu)


def grad_order(experts):
    ids = jnp.arange(FETCH, dtype=jnp.int32)
    own = jnp.arange(EXP_GROUP, dtype=jnp.int32)
    listed = experts[None, :] == own[:, None]
    first = jnp.min(jnp.where(listed, ids[None, :], FETCH), axis=1)
    first = jnp.where(first == FETCH, 0, first)
    key = jnp.concatenate([own * 32, experts * 32 + 1 + ids])
    chunk = jnp.concatenate([first, ids])
    owner = jnp.concatenate([own, experts])
    rank = jnp.sum((key[None, :] < key[:, None]).astype(jnp.int32), axis=1)
    place = rank[:, None] == jnp.arange(STEPS, dtype=jnp.int32)[None, :]

    def ordered(values):
        return jnp.sum(jnp.where(place, values[:, None], 0), axis=0)

    count = jnp.sum((owner[None, :] == owner[:, None]) & (key[None, :] > key[:, None]), axis=1)
    real = (jnp.arange(STEPS) >= EXP_GROUP).astype(jnp.int32)
    last = (count == 0).astype(jnp.int32)
    return ordered(chunk), ordered(owner), ordered(real), ordered(last)


Z_GROUPS = [[0, 2, 4, 6], [1, 3, 5, 7]]
PAIRS = [(i, i ^ 1) for i in range(8)]


def shards(
    queries, key_rows, value_rows, out_proj, residual, norm_gain, w_gate, w_up, w_down,
    route_slot, route_weight, fetch_list, cotangent,
):
    tokens = queries.shape[0]
    hidden = lax.axis_index("hidden")
    group = lax.axis_index("group")
    core = hidden % 2
    core_arr = core.reshape(1).astype(jnp.int32)

    slot_ids = jnp.arange(FETCH, dtype=jnp.int32)
    chosen = route_slot[:, :, None] == slot_ids[None, None, :]
    slot_weight = jnp.sum(jnp.where(chosen, route_weight[:, :, None], 0.0), axis=1)
    used = jnp.any(chosen, axis=1)
    lower = (
        lax.broadcasted_iota(jnp.int32, (tokens, tokens), 0)
        >= lax.broadcasted_iota(jnp.int32, (tokens, tokens), 1)
    ).astype(bf16)
    position = mm(lower, used.astype(bf16), NN).astype(jnp.int32) - 1
    position = jnp.where(used, position, -1)
    pos_t, weight_t = position.T, slot_weight.T
    caps = jnp.arange(CAP, dtype=jnp.int32)
    hit = pos_t[:, None, :] == caps[None, :, None]
    pick = hit.astype(bf16).reshape(FETCH * CAP, tokens)
    row_weight = jnp.sum(jnp.where(hit, weight_t[:, None, :], 0.0), axis=2).reshape(-1, 1)

    cot_half = lax.dynamic_slice_in_dim(cotangent, core * HALF, HALF, 1)
    grad_rows = (mm(pick, cot_half, NN) * row_weight).astype(bf16)
    g_own = lax.all_to_all(
        grad_rows.reshape(FETCH, CAP, HALF), "group", split_axis=0, concat_axis=0, tiled=True
    )
    g_oth = lax.ppermute(g_own, "hidden", PAIRS)

    kv = hidden * (queries.shape[1] // HEAD_DIM) // (HEADS // KV_HEADS)
    key_block = lax.dynamic_slice_in_dim(key_rows, kv * HEAD_DIM, HEAD_DIM, 1)
    value_block = lax.dynamic_slice_in_dim(value_rows, kv * HEAD_DIM, HEAD_DIM, 1)
    mixed = attention(queries, key_block, value_block)
    proj = out_proj.reshape(out_proj.shape[0], 8, COLS)
    part = jnp.einsum("tk,khc->htc", mixed, proj, preferred_element_type=f32).astype(bf16)
    parts = lax.all_to_all(part, "hidden", split_axis=0, concat_axis=0, tiled=True)
    first_col = hidden * COLS
    res_share = lax.dynamic_slice_in_dim(residual, first_col, COLS, 1)
    gain = lax.dynamic_slice_in_dim(norm_gain, first_col, COLS, 0)
    stream = res_share.astype(f32) + jnp.sum(parts.astype(f32), axis=0)
    square = lax.psum(jnp.sum(stream * stream, axis=1), "hidden") / D
    normed = (stream * lax.rsqrt(square + epsilon)[:, None] * gain[None, :]).astype(bf16)

    x_part = mm(pick, normed, NN).astype(bf16).reshape(FETCH, CAP, COLS)
    x_part = lax.all_to_all(x_part, "group", split_axis=0, concat_axis=0, tiled=True)
    x_rows = lax.all_gather(x_part, "hidden", axis=0, tiled=False)

    own_col = lax.dynamic_slice_in_dim(fetch_list, group, 1, 1)[:, 0]
    experts = own_col - group * EXP_GROUP
    wg, wu = w_gate.transpose(0, 2, 1), w_up.transpose(0, 2, 1)
    out_rows, d_own, d_oth, act, dgu = rows_call(
        experts, core_arr, x_rows, g_own, g_oth, wg, wu, w_down
    )

    out_share = lax.psum_scatter(
        out_rows, "hidden", scatter_dimension=0, tiled=True
    ).reshape(FETCH, CAP, COLS)
    out_back = lax.all_to_all(out_share, "group", split_axis=0, concat_axis=0, tiled=True)
    d_in = lax.ppermute(d_oth, "hidden", PAIRS)
    d_sum = (d_own.astype(f32) + d_in.astype(f32)).astype(bf16)
    d_back = lax.all_to_all(d_sum, "group", split_axis=0, concat_axis=0, tiled=True)

    chunk, expert, real, last = grad_order(experts)
    grad_gate, grad_up, grad_down = grads_call(
        chunk, expert, real, last, core_arr, x_rows, g_own, g_oth, act, dgu
    )

    d_tok = mm(pick, d_back.reshape(FETCH * CAP, HALF), TN).astype(bf16)
    d_tok = d_tok.reshape(tokens, 4, COLS).transpose(1, 0, 2)
    d_parts = lax.all_to_all(
        d_tok, "hidden", split_axis=0, concat_axis=0, tiled=True, axis_index_groups=Z_GROUPS
    )
    grad_normed = jnp.sum(d_parts.astype(f32), axis=0).astype(bf16)

    high = row_weight.astype(bf16)
    low = (row_weight - high.astype(f32)).astype(bf16)
    out_flat = out_back.reshape(FETCH * CAP, COLS)
    moe = mm(pick * high, out_flat, TN) + mm(pick * low, out_flat, TN)
    layer_out = (stream + moe).astype(bf16)
    return (
        layer_out,
        grad_normed,
        grad_gate.transpose(0, 2, 1),
        grad_up.transpose(0, 2, 1),
        grad_down,
    )


def solution(mesh):
    return jax.shard_map(
        shards,
        mesh=mesh,
        in_specs=(
            P("group", "hidden"),
            P("group", None),
            P("group", None),
            P("hidden", None),
            P("group", None),
            P(),
            P("group", None, "hidden"),
            P("group", None, "hidden"),
            P("group", "hidden", None),
            P("group", None),
            P("group", None),
            P(),
            P("group", None),
        ),
        out_specs=(
            P("group", "hidden"),
            P("group", "hidden"),
            P("group", None, "hidden"),
            P("group", None, "hidden"),
            P("group", "hidden", None),
        ),
        check_vma=False,
    )
```

```python
import math

import jax
import jax.numpy as jnp
from jax import lax
from jax.experimental import pallas as pl
from jax.experimental.pallas import tpu as pltpu
from jax.sharding import PartitionSpec as P

D = 2048
HEADS = 32
KV_HEADS = 4
HEAD_DIM = 128
EXP_GROUP = 8
FETCH = 16
CAP = 240
UNITS = 96
PAD = 128
COLS = 256
HALF = 1024
STEPS = FETCH + EXP_GROUP
SPLIT = (96, 144)

epsilon = 1e-06
bf16 = jnp.bfloat16
f32 = jnp.float32

NT = (((1,), (1,)), ((), ()))
NN = (((1,), (0,)), ((), ()))
TN = (((0,), (0,)), ((), ()))


def mm(a, b, dims):
    return lax.dot_general(a, b, dims, preferred_element_type=f32)


def attention(queries, key_block, value_block):
    tokens = queries.shape[0]
    heads = queries.shape[1] // HEAD_DIM
    query = queries.reshape(tokens, heads, HEAD_DIM)
    scores = jnp.einsum("thd,sd->hts", query, key_block, preferred_element_type=f32)
    scores = scores / math.sqrt(HEAD_DIM)
    row_pos = lax.broadcasted_iota(jnp.int32, (tokens, tokens), 0)
    col_pos = lax.broadcasted_iota(jnp.int32, (tokens, tokens), 1)
    scores = jnp.where(row_pos >= col_pos, scores, -1e30)
    weights = jnp.exp(scores - jnp.max(scores, axis=-1, keepdims=True))
    probs = (weights / jnp.sum(weights, axis=-1, keepdims=True)).astype(bf16)
    mixed = jnp.einsum("hts,sd->thd", probs, value_block, preferred_element_type=f32)
    return mixed.astype(bf16).reshape(tokens, heads * HEAD_DIM)


def rows_kernel(expert_ref, core_ref, x_ref, *refs):
    g_refs = refs[: 2 * len(SPLIT)]
    wg_ref, wu_ref, wd_ref, out_ref, act_ref, dgu_ref, wgu, wdp = refs[2 * len(SPLIT) :]
    core = core_ref[0]

    @pl.when(pl.program_id(0) == 0)
    def _():
        zeros = jnp.zeros((PAD - UNITS, D), bf16)
        wgu[UNITS:PAD, :] = zeros
        wgu[PAD + UNITS :, :] = zeros
        wdp[UNITS:, :] = zeros

    wgu[:UNITS, :] = wg_ref[0]
    wgu[PAD : PAD + UNITS, :] = wu_ref[0]
    wdp[:UNITS, :] = wd_ref[0]

    pre = mm(x_ref[0, 0], wgu[:, :COLS], NT)
    for block in range(1, D // COLS):
        pre = pre + mm(x_ref[block, 0], wgu[:, block * COLS : (block + 1) * COLS], NT)
    gate, up = pre[:, :PAD], pre[:, PAD:]
    sig = jax.nn.sigmoid(gate)
    swish = gate * sig
    act = (swish * up).astype(bf16)
    act_ref[0] = act
    for block in range(D // COLS):
        out_ref[block, 0] = mm(act, wdp[:, block * COLS : (block + 1) * COLS], NN).astype(bf16)
    own = pl.multiple_of(core * HALF, HALF)
    oth = pl.multiple_of(HALF - core * HALF, HALF)
    start = 0
    for i, size in enumerate(SPLIT):
        d_act = mm(g_refs[2 * i][0], wdp[:, pl.ds(own, HALF)], NT)
        d_act = d_act + mm(g_refs[2 * i + 1][0], wdp[:, pl.ds(oth, HALF)], NT)
        rows = slice(start, start + size)
        gate_i, up_i, sig_i, swish_i = gate[rows], up[rows], sig[rows], swish[rows]
        dgu_ref[0, rows, :PAD] = (
            d_act * up_i * sig_i * (1.0 + gate_i * (1.0 - sig_i))
        ).astype(bf16)
        dgu_ref[0, rows, PAD:] = (d_act * swish_i).astype(bf16)
        start += size


def rows_call(experts, core, x_rows, g_parts, wg, wu, wd):
    weight = pl.BlockSpec((1, UNITS, D), lambda i, e, c: (e[i], 0, 0))
    cols8 = pl.BlockSpec((8, 1, CAP, COLS), lambda i, e, c: (0, i, 0, 0))

    def flat(size, width):
        return pl.BlockSpec((1, size, width), lambda i, e, c: (i, 0, 0))

    halves = [flat(size, HALF) for size in SPLIT for _ in range(2)]
    return pl.pallas_call(
        rows_kernel,
        grid_spec=pltpu.PrefetchScalarGridSpec(
            num_scalar_prefetch=2,
            grid=(FETCH,),
            in_specs=[cols8, *halves, weight, weight, weight],
            out_specs=[cols8, flat(CAP, PAD), flat(CAP, 2 * PAD)],
            scratch_shapes=[pltpu.VMEM((2 * PAD, D), bf16), pltpu.VMEM((PAD, D), bf16)],
        ),
        out_shape=[
            jax.ShapeDtypeStruct((8, FETCH, CAP, COLS), bf16),
            jax.ShapeDtypeStruct((FETCH, CAP, PAD), bf16),
            jax.ShapeDtypeStruct((FETCH, CAP, 2 * PAD), bf16),
        ],
        compiler_params=pltpu.CompilerParams(vmem_limit_bytes=32 << 20),
        cost_estimate=pl.CostEstimate(
            flops=2 * 4 * FETCH * CAP * D * PAD, bytes_accessed=65 << 20, transcendentals=0
        ),
        name="expert_rows",
    )(experts, core, x_rows, *g_parts, wg, wu, wd)


def input_kernel(
    expert_ref, core_ref, own_ref, oth_ref, wg_ref, wu_ref, wg_oth_ref, wu_oth_ref,
    d_ref, w_own, w_oth,
):
    core = core_ref[0]

    @pl.when(pl.program_id(0) == 0)
    def _():
        zeros = jnp.zeros((PAD - UNITS, HALF), bf16)
        for ref in (w_own, w_oth):
            ref[UNITS:PAD, :] = zeros
            ref[PAD + UNITS :, :] = zeros

    own, oth = own_ref[0], oth_ref[0]
    for block in range(HALF // COLS):
        place = slice(block * COLS, (block + 1) * COLS)
        col = pl.ds(pl.multiple_of((2 * block + core) * COLS, COLS), COLS)
        w_own[:UNITS, place] = wg_ref[0, :, col]
        w_own[PAD : PAD + UNITS, place] = wu_ref[0, :, col]
        w_oth[:UNITS, place] = wg_oth_ref[0, :, col]
        w_oth[PAD : PAD + UNITS, place] = wu_oth_ref[0, :, col]
        d_ref[0, :, place] = (mm(own, w_own[:, place], NN) + mm(oth, w_oth[:, place], NN)).astype(
            bf16
        )


def input_call(experts, core, dgu, dgu_oth, wg, wu, wg_oth, wu_oth):
    weight = pl.BlockSpec((1, UNITS, D), lambda i, e, c: (e[i], 0, 0))
    flat = pl.BlockSpec((1, CAP, 2 * PAD), lambda i, e, c: (i, 0, 0))
    return pl.pallas_call(
        input_kernel,
        grid_spec=pltpu.PrefetchScalarGridSpec(
            num_scalar_prefetch=2,
            grid=(FETCH,),
            in_specs=[flat, flat, weight, weight, weight, weight],
            out_specs=pl.BlockSpec((1, CAP, HALF), lambda i, e, c: (i, 0, 0)),
            scratch_shapes=[pltpu.VMEM((2 * PAD, HALF), bf16)] * 2,
        ),
        out_shape=jax.ShapeDtypeStruct((FETCH, CAP, HALF), bf16),
        compiler_params=pltpu.CompilerParams(vmem_limit_bytes=32 << 20),
        cost_estimate=pl.CostEstimate(
            flops=2 * 2 * FETCH * CAP * D * PAD, bytes_accessed=40 << 20, transcendentals=0
        ),
        name="input_rows",
    )(experts, core, dgu, dgu_oth, wg, wu, wg_oth, wu_oth)


def grads_kernel(chunk_ref, expert_ref, real_ref, last_ref, core_ref, x_ref, *refs):
    g_refs = refs[: 2 * len(SPLIT)]
    act_ref, dgu_ref, gg_ref, gu_ref, gd_ref, acc_gu, acc_d = refs[2 * len(SPLIT) :]
    step = pl.program_id(0)
    core = core_ref[0]

    @pl.when(real_ref[step] == 0)
    def _():
        acc_gu[...] = jnp.zeros_like(acc_gu)
        acc_d[...] = jnp.zeros_like(acc_d)

    @pl.when(real_ref[step] == 1)
    def _():
        d_gu, act = dgu_ref[0], act_ref[0]
        for block in range(D // COLS):
            place = slice(block * COLS, (block + 1) * COLS)
            acc_gu[:, place] += mm(d_gu, x_ref[block, 0], TN)
        start = 0
        for i, size in enumerate(SPLIT):
            act_i = act[start : start + size]
            start += size
            for block in range(HALF // COLS):
                place = slice(block * COLS, (block + 1) * COLS)
                for half, base in ((0, core * HALF), (1, HALF - core * HALF)):
                    col = pl.ds(pl.multiple_of(base + block * COLS, COLS), COLS)
                    acc_d[:, col] += mm(act_i, g_refs[2 * i + half][0, :, place], TN)

    @pl.when(last_ref[step] == 1)
    def _():
        gg_ref[0] = acc_gu[:UNITS, :].astype(bf16)
        gu_ref[0] = acc_gu[PAD : PAD + UNITS, :].astype(bf16)
        gd_ref[0] = acc_d[:UNITS, :].astype(bf16)


def grads_call(chunk, expert, real, last, core, x_rows, g_parts, act, dgu):
    weight = pl.BlockSpec((1, UNITS, D), lambda i, k, e, r, l, c: (e[i], 0, 0))

    def flat(size, width):
        return pl.BlockSpec((1, size, width), lambda i, k, e, r, l, c: (k[i], 0, 0))

    halves = [flat(size, HALF) for size in SPLIT for _ in range(2)]
    return pl.pallas_call(
        grads_kernel,
        grid_spec=pltpu.PrefetchScalarGridSpec(
            num_scalar_prefetch=5,
            grid=(STEPS,),
            in_specs=[
                pl.BlockSpec((8, 1, CAP, COLS), lambda i, k, e, r, l, c: (0, k[i], 0, 0)),
                *halves,
                flat(CAP, PAD),
                flat(CAP, 2 * PAD),
            ],
            out_specs=[weight, weight, weight],
            scratch_shapes=[pltpu.VMEM((2 * PAD, D), f32), pltpu.VMEM((PAD, D), f32)],
        ),
        out_shape=[jax.ShapeDtypeStruct((EXP_GROUP, UNITS, D), bf16)] * 3,
        compiler_params=pltpu.CompilerParams(vmem_limit_bytes=32 << 20),
        cost_estimate=pl.CostEstimate(
            flops=2 * 3 * FETCH * CAP * D * PAD, bytes_accessed=45 << 20, transcendentals=0
        ),
        name="weight_grads",
    )(chunk, expert, real, last, core, x_rows, *g_parts, act, dgu)


def grad_order(experts):
    ids = jnp.arange(FETCH, dtype=jnp.int32)
    own = jnp.arange(EXP_GROUP, dtype=jnp.int32)
    listed = experts[None, :] == own[:, None]
    first = jnp.min(jnp.where(listed, ids[None, :], FETCH), axis=1)
    first = jnp.where(first == FETCH, 0, first)
    key = jnp.concatenate([own * 32, experts * 32 + 1 + ids])
    chunk = jnp.concatenate([first, ids])
    owner = jnp.concatenate([own, experts])
    rank = jnp.sum((key[None, :] < key[:, None]).astype(jnp.int32), axis=1)
    place = rank[:, None] == jnp.arange(STEPS, dtype=jnp.int32)[None, :]

    def ordered(values):
        return jnp.sum(jnp.where(place, values[:, None], 0), axis=0)

    count = jnp.sum((owner[None, :] == owner[:, None]) & (key[None, :] > key[:, None]), axis=1)
    real = (jnp.arange(STEPS) >= EXP_GROUP).astype(jnp.int32)
    last = (count == 0).astype(jnp.int32)
    return ordered(chunk), ordered(owner), ordered(real), ordered(last)


Z_GROUPS = [[0, 2, 4, 6], [1, 3, 5, 7]]
PAIRS = [(i, i ^ 1) for i in range(8)]


def after(value, *others):
    return lax.optimization_barrier((value,) + others)[0]


def exchange(value, axis="group"):
    return lax.all_to_all(value, axis, split_axis=0, concat_axis=0, tiled=True)


def swap(value):
    return lax.ppermute(value, "hidden", PAIRS)


def shards(
    queries, key_rows, value_rows, out_proj, residual, norm_gain, w_gate, w_up, w_down,
    route_slot, route_weight, fetch_list, cotangent,
):
    tokens = queries.shape[0]
    hidden = lax.axis_index("hidden")
    group = lax.axis_index("group")
    core = hidden % 2
    core_arr = core.reshape(1).astype(jnp.int32)
    wg, wu = w_gate.transpose(0, 2, 1), w_up.transpose(0, 2, 1)
    wg_oth, wu_oth = swap(wg), swap(wu)

    kv = hidden * (queries.shape[1] // HEAD_DIM) // (HEADS // KV_HEADS)
    key_block = lax.dynamic_slice_in_dim(key_rows, kv * HEAD_DIM, HEAD_DIM, 1)
    value_block = lax.dynamic_slice_in_dim(value_rows, kv * HEAD_DIM, HEAD_DIM, 1)
    mixed = attention(queries, key_block, value_block)
    proj = out_proj.reshape(out_proj.shape[0], 8, COLS)
    part = jnp.einsum("tk,khc->htc", mixed, proj, preferred_element_type=f32).astype(bf16)
    attn = lax.psum_scatter(part, "hidden", scatter_dimension=0, tiled=True)[0]

    route_slot = after(route_slot, part)
    slot_ids = jnp.arange(FETCH, dtype=jnp.int32)
    chosen = route_slot[:, :, None] == slot_ids[None, None, :]
    slot_weight = jnp.sum(jnp.where(chosen, route_weight[:, :, None], 0.0), axis=1)
    used = jnp.any(chosen, axis=1)
    lower = (
        lax.broadcasted_iota(jnp.int32, (tokens, tokens), 0)
        >= lax.broadcasted_iota(jnp.int32, (tokens, tokens), 1)
    ).astype(bf16)
    position = mm(lower, used.astype(bf16), NN).astype(jnp.int32) - 1
    position = jnp.where(used, position, -1)
    pos_t, weight_t = position.T, slot_weight.T

    def one_hot(start, size):
        caps = start + jnp.arange(size, dtype=jnp.int32)
        hit = pos_t[:, None, :] == caps[None, :, None]
        weight = jnp.sum(jnp.where(hit, weight_t[:, None, :], 0.0), axis=2)
        return hit.astype(bf16).reshape(FETCH * size, tokens), weight.reshape(-1, 1)

    cot_half = lax.dynamic_slice_in_dim(cotangent, core * HALF, HALF, 1)

    def grad_rows(start, size):
        pick, weight = one_hot(start, size)
        return (mm(pick, cot_half, NN) * weight).astype(bf16).reshape(FETCH, size, HALF)

    g_first = exchange(after(grad_rows(0, SPLIT[0]), wg_oth, wu_oth))

    first_col = hidden * COLS
    res_share = lax.dynamic_slice_in_dim(residual, first_col, COLS, 1)
    gain = lax.dynamic_slice_in_dim(norm_gain, first_col, COLS, 0)
    stream = res_share.astype(f32) + attn.astype(f32)
    square = lax.psum(jnp.sum(stream * stream, axis=1), "hidden") / D
    normed = (stream * lax.rsqrt(square + epsilon)[:, None] * gain[None, :]).astype(bf16)

    pick, row_weight = one_hot(0, CAP)
    x_part = mm(pick, normed, NN).astype(bf16).reshape(FETCH, CAP, COLS)
    x_part = exchange(after(x_part, g_first))
    x_rows = lax.all_gather(x_part, "hidden", axis=0, tiled=False)
    g_second = exchange(after(grad_rows(SPLIT[0], SPLIT[1]), x_part))
    g_parts = [g_first, swap(g_first), g_second, swap(g_second)]

    own_col = lax.dynamic_slice_in_dim(fetch_list, group, 1, 1)[:, 0]
    experts = own_col - group * EXP_GROUP
    out_rows, act, dgu = rows_call(experts, core_arr, x_rows, g_parts, wg, wu, w_down)
    d_half = input_call(experts, core_arr, dgu, swap(dgu), wg, wu, wg_oth, wu_oth)

    out_share = lax.psum_scatter(out_rows, "hidden", scatter_dimension=0, tiled=True)[0]
    d_back = exchange(d_half)
    chunk, expert, real, last = grad_order(experts)
    grad_gate, grad_up, grad_down = grads_call(
        chunk, expert, real, last, core_arr, x_rows, g_parts, act, dgu
    )
    out_back = exchange(after(out_share, d_back))

    d_tok = mm(pick, d_back.reshape(-1, HALF), TN).astype(bf16)
    d_tok = d_tok.reshape(tokens, 4, COLS).transpose(1, 0, 2)
    grad_normed = lax.psum_scatter(
        d_tok, "hidden", scatter_dimension=0, tiled=True, axis_index_groups=Z_GROUPS
    )[0]

    high = row_weight.astype(bf16)
    low = (row_weight - high.astype(f32)).astype(bf16)
    out_back = out_back.reshape(-1, COLS)
    moe = mm(pick * high, out_back, TN) + mm(pick * low, out_back, TN)
    layer_out = (stream + moe).astype(bf16)
    return (
        layer_out,
        grad_normed,
        grad_gate.transpose(0, 2, 1),
        grad_up.transpose(0, 2, 1),
        grad_down,
    )


def solution(mesh):
    return jax.shard_map(
        shards,
        mesh=mesh,
        in_specs=(
            P("group", "hidden"),
            P("group", None),
            P("group", None),
            P("hidden", None),
            P("group", None),
            P(),
            P("group", None, "hidden"),
            P("group", None, "hidden"),
            P("group", "hidden", None),
            P("group", None),
            P("group", None),
            P(),
            P("group", None),
        ),
        out_specs=(
            P("group", "hidden"),
            P("group", "hidden"),
            P("group", None, "hidden"),
            P("group", None, "hidden"),
            P("group", "hidden", None),
        ),
        check_vma=False,
    )
```

```python
import math

import jax
import jax.numpy as jnp
from jax import lax
from jax.experimental import pallas as pl
from jax.experimental.pallas import tpu as pltpu
from jax.sharding import PartitionSpec as P

D = 2048
HEADS = 32
KV_HEADS = 4
HEAD_DIM = 128
EXP_GROUP = 8
FETCH = 16
CAP = 240
UNITS = 96
PAD = 128
COLS = 256
HALF = 1024
STEPS = FETCH + EXP_GROUP
SPLIT = (64, 176)

epsilon = 1e-06
bf16 = jnp.bfloat16
f32 = jnp.float32

NT = (((1,), (1,)), ((), ()))
NN = (((1,), (0,)), ((), ()))
TN = (((0,), (0,)), ((), ()))


def mm(a, b, dims):
    return lax.dot_general(a, b, dims, preferred_element_type=f32)


def attention(queries, key_block, value_block):
    tokens = queries.shape[0]
    heads = queries.shape[1] // HEAD_DIM
    query = queries.reshape(tokens, heads, HEAD_DIM)
    scores = jnp.einsum("thd,sd->hts", query, key_block, preferred_element_type=f32)
    scores = scores / math.sqrt(HEAD_DIM)
    row_pos = lax.broadcasted_iota(jnp.int32, (tokens, tokens), 0)
    col_pos = lax.broadcasted_iota(jnp.int32, (tokens, tokens), 1)
    scores = jnp.where(row_pos >= col_pos, scores, -1e30)
    weights = jnp.exp(scores - jnp.max(scores, axis=-1, keepdims=True))
    probs = (weights / jnp.sum(weights, axis=-1, keepdims=True)).astype(bf16)
    mixed = jnp.einsum("hts,sd->thd", probs, value_block, preferred_element_type=f32)
    return mixed.astype(bf16).reshape(tokens, heads * HEAD_DIM)


def rows_kernel(order_ref, expert_ref, fresh_ref, core_ref, x_ref, *refs):
    g_refs = refs[: 2 * len(SPLIT)]
    wg_ref, wu_ref, wd_ref, out_ref, act_ref, dgu_ref, wgu, wdp = refs[2 * len(SPLIT) :]
    core = core_ref[0]

    @pl.when(pl.program_id(0) == 0)
    def _():
        zeros = jnp.zeros((PAD - UNITS, D), bf16)
        wgu[UNITS:PAD, :] = zeros
        wgu[PAD + UNITS :, :] = zeros
        wdp[UNITS:, :] = zeros

    @pl.when(fresh_ref[pl.program_id(0)] == 1)
    def _():
        wgu[:UNITS, :] = wg_ref[0]
        wgu[PAD : PAD + UNITS, :] = wu_ref[0]
        wdp[:UNITS, :] = wd_ref[0]

    pre = mm(x_ref[0, 0], wgu[:, :COLS], NT)
    for block in range(1, D // COLS):
        pre = pre + mm(x_ref[block, 0], wgu[:, block * COLS : (block + 1) * COLS], NT)
    gate, up = pre[:, :PAD], pre[:, PAD:]
    sig = jax.nn.sigmoid(gate)
    swish = gate * sig
    act = (swish * up).astype(bf16)
    act_ref[0] = act
    for block in range(D // COLS):
        out_ref[block, 0] = mm(act, wdp[:, block * COLS : (block + 1) * COLS], NN).astype(bf16)
    own = pl.multiple_of(core * HALF, HALF)
    oth = pl.multiple_of(HALF - core * HALF, HALF)
    start = 0
    for i, size in enumerate(SPLIT):
        d_act = mm(g_refs[2 * i][0], wdp[:, pl.ds(own, HALF)], NT)
        d_act = d_act + mm(g_refs[2 * i + 1][0], wdp[:, pl.ds(oth, HALF)], NT)
        rows = slice(start, start + size)
        gate_i, up_i, sig_i, swish_i = gate[rows], up[rows], sig[rows], swish[rows]
        dgu_ref[0, rows, :PAD] = (
            d_act * up_i * sig_i * (1.0 + gate_i * (1.0 - sig_i))
        ).astype(bf16)
        dgu_ref[0, rows, PAD:] = (d_act * swish_i).astype(bf16)
        start += size


def rows_call(scalars, x_rows, g_parts, wg, wu, wd):
    weight = pl.BlockSpec((1, UNITS, D), lambda i, o, e, n, c: (e[i], 0, 0))
    cols8 = pl.BlockSpec((8, 1, CAP, COLS), lambda i, o, e, n, c: (0, o[i], 0, 0))

    def flat(size, width):
        return pl.BlockSpec((1, size, width), lambda i, o, e, n, c: (o[i], 0, 0))

    halves = [flat(size, HALF) for size in SPLIT for _ in range(2)]
    return pl.pallas_call(
        rows_kernel,
        grid_spec=pltpu.PrefetchScalarGridSpec(
            num_scalar_prefetch=4,
            grid=(FETCH,),
            in_specs=[cols8, *halves, weight, weight, weight],
            out_specs=[cols8, flat(CAP, PAD), flat(CAP, 2 * PAD)],
            scratch_shapes=[pltpu.VMEM((2 * PAD, D), bf16), pltpu.VMEM((PAD, D), bf16)],
        ),
        out_shape=[
            jax.ShapeDtypeStruct((8, FETCH, CAP, COLS), bf16),
            jax.ShapeDtypeStruct((FETCH, CAP, PAD), bf16),
            jax.ShapeDtypeStruct((FETCH, CAP, 2 * PAD), bf16),
        ],
        compiler_params=pltpu.CompilerParams(vmem_limit_bytes=56 << 20),
        cost_estimate=pl.CostEstimate(
            flops=2 * 4 * FETCH * CAP * D * PAD, bytes_accessed=65 << 20, transcendentals=0
        ),
        name="expert_rows",
    )(*scalars, x_rows, *g_parts, wg, wu, wd)


def input_kernel(
    order_ref, expert_ref, fresh_ref, core_ref, own_ref, oth_ref, wg_ref, wu_ref, wg_oth_ref, wu_oth_ref,
    d_ref, w_own, w_oth,
):
    core = core_ref[0]

    @pl.when(pl.program_id(0) == 0)
    def _():
        zeros = jnp.zeros((PAD - UNITS, HALF), bf16)
        for ref in (w_own, w_oth):
            ref[UNITS:PAD, :] = zeros
            ref[PAD + UNITS :, :] = zeros

    @pl.when(fresh_ref[pl.program_id(0)] == 1)
    def _():
        for block in range(HALF // COLS):
            place = slice(block * COLS, (block + 1) * COLS)
            col = pl.ds(pl.multiple_of((2 * block + core) * COLS, COLS), COLS)
            w_own[:UNITS, place] = wg_ref[0, :, col]
            w_own[PAD : PAD + UNITS, place] = wu_ref[0, :, col]
            w_oth[:UNITS, place] = wg_oth_ref[0, :, col]
            w_oth[PAD : PAD + UNITS, place] = wu_oth_ref[0, :, col]

    own, oth = own_ref[0], oth_ref[0]
    for block in range(HALF // COLS):
        place = slice(block * COLS, (block + 1) * COLS)
        d_ref[0, :, place] = (mm(own, w_own[:, place], NN) + mm(oth, w_oth[:, place], NN)).astype(
            bf16
        )


def input_call(scalars, dgu, dgu_oth, wg, wu, wg_oth, wu_oth):
    weight = pl.BlockSpec((1, UNITS, D), lambda i, o, e, n, c: (e[i], 0, 0))
    flat = pl.BlockSpec((1, CAP, 2 * PAD), lambda i, o, e, n, c: (o[i], 0, 0))
    return pl.pallas_call(
        input_kernel,
        grid_spec=pltpu.PrefetchScalarGridSpec(
            num_scalar_prefetch=4,
            grid=(FETCH,),
            in_specs=[flat, flat, weight, weight, weight, weight],
            out_specs=pl.BlockSpec((1, CAP, HALF), lambda i, o, e, n, c: (o[i], 0, 0)),
            scratch_shapes=[pltpu.VMEM((2 * PAD, HALF), bf16)] * 2,
        ),
        out_shape=jax.ShapeDtypeStruct((FETCH, CAP, HALF), bf16),
        compiler_params=pltpu.CompilerParams(vmem_limit_bytes=56 << 20),
        cost_estimate=pl.CostEstimate(
            flops=2 * 2 * FETCH * CAP * D * PAD, bytes_accessed=40 << 20, transcendentals=0
        ),
        name="input_rows",
    )(*scalars, dgu, dgu_oth, wg, wu, wg_oth, wu_oth)


def grads_kernel(chunk_ref, expert_ref, real_ref, last_ref, core_ref, x_ref, *refs):
    g_refs = refs[: 2 * len(SPLIT)]
    act_ref, dgu_ref, gg_ref, gu_ref, gd_ref, acc_gu, acc_d = refs[2 * len(SPLIT) :]
    step = pl.program_id(0)
    core = core_ref[0]

    @pl.when(real_ref[step] == 0)
    def _():
        acc_gu[...] = jnp.zeros_like(acc_gu)
        acc_d[...] = jnp.zeros_like(acc_d)

    @pl.when(real_ref[step] == 1)
    def _():
        d_gu, act = dgu_ref[0], act_ref[0]
        for block in range(D // COLS):
            place = slice(block * COLS, (block + 1) * COLS)
            acc_gu[:, place] += mm(d_gu, x_ref[block, 0], TN)
        start = 0
        for i, size in enumerate(SPLIT):
            act_i = act[start : start + size]
            start += size
            for block in range(HALF // COLS):
                place = slice(block * COLS, (block + 1) * COLS)
                for half, base in ((0, core * HALF), (1, HALF - core * HALF)):
                    col = pl.ds(pl.multiple_of(base + block * COLS, COLS), COLS)
                    acc_d[:, col] += mm(act_i, g_refs[2 * i + half][0, :, place], TN)

    @pl.when(last_ref[step] == 1)
    def _():
        gg_ref[0] = acc_gu[:UNITS, :].astype(bf16)
        gu_ref[0] = acc_gu[PAD : PAD + UNITS, :].astype(bf16)
        gd_ref[0] = acc_d[:UNITS, :].astype(bf16)


def grads_call(chunk, expert, real, last, core, x_rows, g_parts, act, dgu):
    weight = pl.BlockSpec((1, UNITS, D), lambda i, k, e, r, l, c: (e[i], 0, 0))

    def flat(size, width):
        return pl.BlockSpec((1, size, width), lambda i, k, e, r, l, c: (k[i], 0, 0))

    halves = [flat(size, HALF) for size in SPLIT for _ in range(2)]
    return pl.pallas_call(
        grads_kernel,
        grid_spec=pltpu.PrefetchScalarGridSpec(
            num_scalar_prefetch=5,
            grid=(STEPS,),
            in_specs=[
                pl.BlockSpec((8, 1, CAP, COLS), lambda i, k, e, r, l, c: (0, k[i], 0, 0)),
                *halves,
                flat(CAP, PAD),
                flat(CAP, 2 * PAD),
            ],
            out_specs=[weight, weight, weight],
            scratch_shapes=[pltpu.VMEM((2 * PAD, D), f32), pltpu.VMEM((PAD, D), f32)],
        ),
        out_shape=[jax.ShapeDtypeStruct((EXP_GROUP, UNITS, D), bf16)] * 3,
        compiler_params=pltpu.CompilerParams(vmem_limit_bytes=56 << 20),
        cost_estimate=pl.CostEstimate(
            flops=2 * 3 * FETCH * CAP * D * PAD, bytes_accessed=45 << 20, transcendentals=0
        ),
        name="weight_grads",
    )(chunk, expert, real, last, core, x_rows, *g_parts, act, dgu)


def grad_order(experts):
    ids = jnp.arange(FETCH, dtype=jnp.int32)
    own = jnp.arange(EXP_GROUP, dtype=jnp.int32)
    listed = experts[None, :] == own[:, None]
    first = jnp.min(jnp.where(listed, ids[None, :], FETCH), axis=1)
    first = jnp.where(first == FETCH, 0, first)
    key = jnp.concatenate([own * 32, experts * 32 + 1 + ids])
    chunk = jnp.concatenate([first, ids])
    owner = jnp.concatenate([own, experts])
    rank = jnp.sum((key[None, :] < key[:, None]).astype(jnp.int32), axis=1)
    place = rank[:, None] == jnp.arange(STEPS, dtype=jnp.int32)[None, :]

    def ordered(values):
        return jnp.sum(jnp.where(place, values[:, None], 0), axis=0)

    count = jnp.sum((owner[None, :] == owner[:, None]) & (key[None, :] > key[:, None]), axis=1)
    real = (jnp.arange(STEPS) >= EXP_GROUP).astype(jnp.int32)
    last = (count == 0).astype(jnp.int32)
    return ordered(chunk), ordered(owner), ordered(real), ordered(last)


def rows_order(experts):
    ids = jnp.arange(FETCH, dtype=jnp.int32)
    key = experts * FETCH + ids
    rank = jnp.sum((key[None, :] < key[:, None]).astype(jnp.int32), axis=1)
    place = rank[:, None] == ids[None, :]
    order = jnp.sum(jnp.where(place, ids[:, None], 0), axis=0)
    expert = jnp.sum(jnp.where(place, experts[:, None], 0), axis=0)
    earlier = (experts[None, :] == experts[:, None]) & (ids[None, :] < ids[:, None])
    new = 1 - jnp.any(earlier, axis=1).astype(jnp.int32)
    fresh = jnp.sum(jnp.where(place, new[:, None], 0), axis=0)
    return order, expert, fresh


Z_GROUPS = [[0, 2, 4, 6], [1, 3, 5, 7]]
PAIRS = [(i, i ^ 1) for i in range(8)]


def after(value, *others):
    return lax.optimization_barrier((value,) + others)[0]


def exchange(value, axis="group"):
    return lax.all_to_all(value, axis, split_axis=0, concat_axis=0, tiled=True)


def swap(value):
    return lax.ppermute(value, "hidden", PAIRS)


def shards(
    queries, key_rows, value_rows, out_proj, residual, norm_gain, w_gate, w_up, w_down,
    route_slot, route_weight, fetch_list, cotangent,
):
    tokens = queries.shape[0]
    hidden = lax.axis_index("hidden")
    group = lax.axis_index("group")
    core = hidden % 2
    core_arr = core.reshape(1).astype(jnp.int32)
    wg, wu = w_gate.transpose(0, 2, 1), w_up.transpose(0, 2, 1)
    wg_oth, wu_oth = swap(wg), swap(wu)

    kv = hidden * (queries.shape[1] // HEAD_DIM) // (HEADS // KV_HEADS)
    key_block = lax.dynamic_slice_in_dim(key_rows, kv * HEAD_DIM, HEAD_DIM, 1)
    value_block = lax.dynamic_slice_in_dim(value_rows, kv * HEAD_DIM, HEAD_DIM, 1)
    mixed = attention(queries, key_block, value_block)
    proj = out_proj.reshape(out_proj.shape[0], 8, COLS)
    part = jnp.einsum("tk,khc->htc", mixed, proj, preferred_element_type=f32).astype(bf16)
    attn = lax.psum_scatter(part, "hidden", scatter_dimension=0, tiled=True)[0]

    route_slot = after(route_slot, part)
    slot_ids = jnp.arange(FETCH, dtype=jnp.int32)
    chosen = route_slot[:, :, None] == slot_ids[None, None, :]
    slot_weight = jnp.sum(jnp.where(chosen, route_weight[:, :, None], 0.0), axis=1)
    used = jnp.any(chosen, axis=1)
    lower = (
        lax.broadcasted_iota(jnp.int32, (tokens, tokens), 0)
        >= lax.broadcasted_iota(jnp.int32, (tokens, tokens), 1)
    ).astype(bf16)
    position = mm(lower, used.astype(bf16), NN).astype(jnp.int32) - 1
    position = jnp.where(used, position, -1)
    pos_t, weight_t = position.T, slot_weight.T

    def one_hot(start, size):
        caps = start + jnp.arange(size, dtype=jnp.int32)
        hit = pos_t[:, None, :] == caps[None, :, None]
        weight = jnp.sum(jnp.where(hit, weight_t[:, None, :], 0.0), axis=2)
        return hit.astype(bf16).reshape(FETCH * size, tokens), weight.reshape(-1, 1)

    cot_half = lax.dynamic_slice_in_dim(cotangent, core * HALF, HALF, 1)

    def grad_rows(start, size):
        pick, weight = one_hot(start, size)
        return (mm(pick, cot_half, NN) * weight).astype(bf16).reshape(FETCH, size, HALF)

    pick, row_weight = one_hot(0, CAP)
    g_first = exchange(after(grad_rows(0, SPLIT[0]), wg_oth, wu_oth, pick, row_weight))
    g_first_oth = swap(g_first)

    first_col = hidden * COLS
    res_share = lax.dynamic_slice_in_dim(residual, first_col, COLS, 1)
    gain = lax.dynamic_slice_in_dim(norm_gain, first_col, COLS, 0)
    stream = res_share.astype(f32) + attn.astype(f32)
    square = lax.psum(jnp.sum(stream * stream, axis=1), "hidden") / D
    normed = (stream * lax.rsqrt(square + epsilon)[:, None] * gain[None, :]).astype(bf16)

    x_part = mm(pick, normed, NN).astype(bf16).reshape(FETCH, CAP, COLS)
    x_part = exchange(after(x_part, g_first_oth))
    x_rows = lax.all_gather(x_part, "hidden", axis=0, tiled=False)
    g_second = exchange(after(grad_rows(SPLIT[0], SPLIT[1]), x_part))
    g_parts = [g_first, g_first_oth, g_second, swap(g_second)]

    own_col = lax.dynamic_slice_in_dim(fetch_list, group, 1, 1)[:, 0]
    experts = own_col - group * EXP_GROUP
    scalars = (*rows_order(experts), core_arr)
    tables = grad_order(experts)
    high = row_weight.astype(bf16)
    low = (row_weight - high.astype(f32)).astype(bf16)
    x_rows, high, low, *tables = lax.optimization_barrier((x_rows, high, low, *tables))
    out_rows, act, dgu = rows_call(scalars, x_rows, g_parts, wg, wu, w_down)
    d_half = input_call(scalars, dgu, swap(dgu), wg, wu, wg_oth, wu_oth)

    out_share = lax.psum_scatter(out_rows, "hidden", scatter_dimension=0, tiled=True)[0]
    d_back = exchange(d_half)
    grad_gate, grad_up, grad_down = grads_call(
        *tables, core_arr, x_rows, g_parts, after(act, d_back), dgu
    )
    out_back = exchange(after(out_share, d_back))

    d_tok = mm(pick, d_back.reshape(-1, HALF), TN).astype(bf16)
    d_tok = d_tok.reshape(tokens, 4, COLS).transpose(1, 0, 2)
    grad_normed = lax.psum_scatter(
        d_tok, "hidden", scatter_dimension=0, tiled=True, axis_index_groups=Z_GROUPS
    )[0]

    out_back = out_back.reshape(-1, COLS)
    moe = mm(pick * high, out_back, TN) + mm(pick * low, out_back, TN)
    layer_out = (stream + moe).astype(bf16)
    return (
        layer_out,
        grad_normed,
        grad_gate.transpose(0, 2, 1),
        grad_up.transpose(0, 2, 1),
        grad_down,
    )


def solution(mesh):
    return jax.shard_map(
        shards,
        mesh=mesh,
        in_specs=(
            P("group", "hidden"),
            P("group", None),
            P("group", None),
            P("hidden", None),
            P("group", None),
            P(),
            P("group", None, "hidden"),
            P("group", None, "hidden"),
            P("group", "hidden", None),
            P("group", None),
            P("group", None),
            P(),
            P("group", None),
        ),
        out_specs=(
            P("group", "hidden"),
            P("group", "hidden"),
            P("group", None, "hidden"),
            P("group", None, "hidden"),
            P("group", "hidden", None),
        ),
        check_vma=False,
    )
```

```python
import math

import jax
import jax.numpy as jnp
from jax import lax
from jax.experimental import pallas as pl
from jax.experimental.pallas import tpu as pltpu
from jax.sharding import PartitionSpec as P

D = 2048
HEADS = 32
KV_HEADS = 4
HEAD_DIM = 128
EXP_GROUP = 8
FETCH = 16
CAP = 240
UNITS = 96
PAD = 128
COLS = 256
HALF = 1024
STEPS = FETCH + EXP_GROUP
SPLIT = (64, 176)

epsilon = 1e-06
bf16 = jnp.bfloat16
f32 = jnp.float32

NT = (((1,), (1,)), ((), ()))
NN = (((1,), (0,)), ((), ()))
TN = (((0,), (0,)), ((), ()))


def mm(a, b, dims):
    return lax.dot_general(a, b, dims, preferred_element_type=f32)


def attention(queries, key_block, value_block):
    tokens = queries.shape[0]
    heads = queries.shape[1] // HEAD_DIM
    query = queries.reshape(tokens, heads, HEAD_DIM)
    scores = jnp.einsum("thd,sd->hts", query, key_block, preferred_element_type=f32)
    scores = scores / math.sqrt(HEAD_DIM)
    row_pos = lax.broadcasted_iota(jnp.int32, (tokens, tokens), 0)
    col_pos = lax.broadcasted_iota(jnp.int32, (tokens, tokens), 1)
    scores = jnp.where(row_pos >= col_pos, scores, -1e30)
    weights = jnp.exp(scores - jnp.max(scores, axis=-1, keepdims=True))
    probs = (weights / jnp.sum(weights, axis=-1, keepdims=True)).astype(bf16)
    mixed = jnp.einsum("hts,sd->thd", probs, value_block, preferred_element_type=f32)
    return mixed.astype(bf16).reshape(tokens, heads * HEAD_DIM)


def rows_kernel(order_ref, expert_ref, fresh_ref, core_ref, x_ref, *refs):
    g_refs = refs[: 2 * len(SPLIT)]
    (
        wg_ref, wu_ref, wd_ref, wg_oth_ref, wu_oth_ref, wd_oth_ref,
        out_ref, act_ref, dgu_ref, d_ref, wgu, wdp,
    ) = refs[2 * len(SPLIT) :]
    step = pl.program_id(0)
    core = core_ref[0]

    @pl.when(step == 0)
    def _():
        for ref in (wgu, wdp):
            for start in range(0, ref.shape[0], PAD):
                ref[start + UNITS : start + PAD, :] = jnp.zeros((PAD - UNITS, D), bf16)

    @pl.when(fresh_ref[step] == 1)
    def _():
        for i, ref in enumerate((wg_ref, wu_ref, wg_oth_ref, wu_oth_ref)):
            wgu[i * PAD : i * PAD + UNITS, :] = ref[0]
        own = pl.ds(pl.multiple_of(core * HALF, HALF), HALF)
        oth = pl.ds(pl.multiple_of(HALF - core * HALF, HALF), HALF)
        for i, ref in enumerate((wd_ref, wd_oth_ref)):
            wdp[i * PAD : i * PAD + UNITS, :HALF] = ref[0, :, own]
            wdp[i * PAD : i * PAD + UNITS, HALF:] = ref[0, :, oth]

    x = jnp.concatenate([x_ref[block, 0] for block in range(D // COLS)], axis=1)
    pre = mm(x, wgu[...], NT)
    g = jnp.concatenate(
        [
            jnp.concatenate([g_refs[2 * i][0], g_refs[2 * i + 1][0]], axis=1)
            for i in range(len(SPLIT))
        ],
        axis=0,
    )
    d_act = mm(g, wdp[...], NT)
    hidden = []
    for i in range(2):
        gate = pre[:, 2 * i * PAD : (2 * i + 1) * PAD]
        up = pre[:, (2 * i + 1) * PAD : (2 * i + 2) * PAD]
        d_part = d_act[:, i * PAD : (i + 1) * PAD]
        sig = jax.nn.sigmoid(gate)
        swish = gate * sig
        if i == 0:
            act = (swish * up).astype(bf16)
        hidden.append((d_part * up * sig * (1.0 + gate * (1.0 - sig))).astype(bf16))
        hidden.append((d_part * swish).astype(bf16))
    act_ref[0] = act
    dgu_ref[0, :, :PAD] = hidden[0]
    dgu_ref[0, :, PAD:] = hidden[1]
    for half, base in enumerate((core * 4, 4 - core * 4)):
        for block in range(4):
            col = half * HALF + block * COLS
            out_ref[base + block, 0] = mm(act, wdp[:PAD, col : col + COLS], NN).astype(bf16)
    both = jnp.concatenate(hidden, axis=1)
    for block in range(4):
        col = pl.ds(pl.multiple_of((2 * block + core) * COLS, COLS), COLS)
        d_ref[0, :, block * COLS : (block + 1) * COLS] = mm(both, wgu[:, col], NN).astype(bf16)


def rows_call(scalars, x_rows, g_parts, weights):
    weight = pl.BlockSpec((1, UNITS, D), lambda i, o, e, n, c: (e[i], 0, 0))
    cols8 = pl.BlockSpec((8, 1, CAP, COLS), lambda i, o, e, n, c: (0, o[i], 0, 0))

    def flat(size, width):
        return pl.BlockSpec((1, size, width), lambda i, o, e, n, c: (o[i], 0, 0))

    halves = [flat(size, HALF) for size in SPLIT for _ in range(2)]
    return pl.pallas_call(
        rows_kernel,
        grid_spec=pltpu.PrefetchScalarGridSpec(
            num_scalar_prefetch=4,
            grid=(FETCH,),
            in_specs=[cols8, *halves, *[weight] * 6],
            out_specs=[cols8, flat(CAP, PAD), flat(CAP, 2 * PAD), flat(CAP, HALF)],
            scratch_shapes=[pltpu.VMEM((4 * PAD, D), bf16), pltpu.VMEM((2 * PAD, D), bf16)],
        ),
        out_shape=[
            jax.ShapeDtypeStruct((8, FETCH, CAP, COLS), bf16),
            jax.ShapeDtypeStruct((FETCH, CAP, PAD), bf16),
            jax.ShapeDtypeStruct((FETCH, CAP, 2 * PAD), bf16),
            jax.ShapeDtypeStruct((FETCH, CAP, HALF), bf16),
        ],
        compiler_params=pltpu.CompilerParams(vmem_limit_bytes=56 << 20),
        cost_estimate=pl.CostEstimate(
            flops=2 * 9 * FETCH * CAP * D * PAD, bytes_accessed=80 << 20, transcendentals=0
        ),
        name="expert_rows",
    )(*scalars, x_rows, *g_parts, *weights)


def grads_kernel(chunk_ref, expert_ref, real_ref, last_ref, core_ref, x_ref, *refs):
    g_refs = refs[: 2 * len(SPLIT)]
    act_ref, dgu_ref, gg_ref, gu_ref, gd_ref, acc_gu, acc_d = refs[2 * len(SPLIT) :]
    step = pl.program_id(0)
    core = core_ref[0]

    @pl.when(real_ref[step] == 0)
    def _():
        acc_gu[...] = jnp.zeros_like(acc_gu)
        acc_d[...] = jnp.zeros_like(acc_d)

    @pl.when(real_ref[step] == 1)
    def _():
        d_gu, act = dgu_ref[0].T, act_ref[0].T
        for block in range(D // COLS):
            place = slice(block * COLS, (block + 1) * COLS)
            acc_gu[:, place] += mm(d_gu, x_ref[block, 0], NN)
        for half in range(2):
            for block in range(HALF // COLS):
                place = slice(block * COLS, (block + 1) * COLS)
                g = jnp.concatenate(
                    [g_refs[2 * i + half][0, :, place] for i in range(len(SPLIT))], axis=0
                )
                col = half * HALF + block * COLS
                acc_d[:, col : col + COLS] += mm(act, g, NN)

    @pl.when(last_ref[step] == 1)
    def _():
        gg_ref[0] = acc_gu[:UNITS, :].astype(bf16)
        gu_ref[0] = acc_gu[PAD : PAD + UNITS, :].astype(bf16)
        for half, base in enumerate((core * HALF, HALF - core * HALF)):
            col = pl.ds(pl.multiple_of(base, HALF), HALF)
            gd_ref[0, :, col] = acc_d[:UNITS, half * HALF : (half + 1) * HALF].astype(bf16)


def grads_call(chunk, expert, real, last, core, x_rows, g_parts, act, dgu):
    weight = pl.BlockSpec((1, UNITS, D), lambda i, k, e, r, l, c: (e[i], 0, 0))

    def flat(size, width):
        return pl.BlockSpec((1, size, width), lambda i, k, e, r, l, c: (k[i], 0, 0))

    halves = [flat(size, HALF) for size in SPLIT for _ in range(2)]
    return pl.pallas_call(
        grads_kernel,
        grid_spec=pltpu.PrefetchScalarGridSpec(
            num_scalar_prefetch=5,
            grid=(STEPS,),
            in_specs=[
                pl.BlockSpec((8, 1, CAP, COLS), lambda i, k, e, r, l, c: (0, k[i], 0, 0)),
                *halves,
                flat(CAP, PAD),
                flat(CAP, 2 * PAD),
            ],
            out_specs=[weight, weight, weight],
            scratch_shapes=[pltpu.VMEM((2 * PAD, D), f32), pltpu.VMEM((PAD, D), f32)],
        ),
        out_shape=[jax.ShapeDtypeStruct((EXP_GROUP, UNITS, D), bf16)] * 3,
        compiler_params=pltpu.CompilerParams(vmem_limit_bytes=56 << 20),
        cost_estimate=pl.CostEstimate(
            flops=2 * 3 * FETCH * CAP * D * PAD, bytes_accessed=45 << 20, transcendentals=0
        ),
        name="weight_grads",
    )(chunk, expert, real, last, core, x_rows, *g_parts, act, dgu)


def grad_order(experts):
    ids = jnp.arange(FETCH, dtype=jnp.int32)
    own = jnp.arange(EXP_GROUP, dtype=jnp.int32)
    listed = experts[None, :] == own[:, None]
    first = jnp.min(jnp.where(listed, ids[None, :], FETCH), axis=1)
    first = jnp.where(first == FETCH, 0, first)
    key = jnp.concatenate([own * 32, experts * 32 + 1 + ids])
    chunk = jnp.concatenate([first, ids])
    owner = jnp.concatenate([own, experts])
    rank = jnp.sum((key[None, :] < key[:, None]).astype(jnp.int32), axis=1)
    place = rank[:, None] == jnp.arange(STEPS, dtype=jnp.int32)[None, :]

    def ordered(values):
        return jnp.sum(jnp.where(place, values[:, None], 0), axis=0)

    count = jnp.sum((owner[None, :] == owner[:, None]) & (key[None, :] > key[:, None]), axis=1)
    real = (jnp.arange(STEPS) >= EXP_GROUP).astype(jnp.int32)
    last = (count == 0).astype(jnp.int32)
    return ordered(chunk), ordered(owner), ordered(real), ordered(last)


def rows_order(experts):
    ids = jnp.arange(FETCH, dtype=jnp.int32)
    key = experts * FETCH + ids
    rank = jnp.sum((key[None, :] < key[:, None]).astype(jnp.int32), axis=1)
    place = rank[:, None] == ids[None, :]
    order = jnp.sum(jnp.where(place, ids[:, None], 0), axis=0)
    expert = jnp.sum(jnp.where(place, experts[:, None], 0), axis=0)
    earlier = (experts[None, :] == experts[:, None]) & (ids[None, :] < ids[:, None])
    new = 1 - jnp.any(earlier, axis=1).astype(jnp.int32)
    fresh = jnp.sum(jnp.where(place, new[:, None], 0), axis=0)
    return order, expert, fresh


Z_GROUPS = [[0, 2, 4, 6], [1, 3, 5, 7]]
PAIRS = [(i, i ^ 1) for i in range(8)]


def after(value, *others):
    return lax.optimization_barrier((value,) + others)[0]


def exchange(value, axis="group"):
    return lax.all_to_all(value, axis, split_axis=0, concat_axis=0, tiled=True)


def swap(value):
    return lax.ppermute(value, "hidden", PAIRS)


def shards(
    queries, key_rows, value_rows, out_proj, residual, norm_gain, w_gate, w_up, w_down,
    route_slot, route_weight, fetch_list, cotangent,
):
    tokens = queries.shape[0]
    hidden = lax.axis_index("hidden")
    group = lax.axis_index("group")
    core = hidden % 2
    core_arr = core.reshape(1).astype(jnp.int32)
    wg, wu = w_gate.transpose(0, 2, 1), w_up.transpose(0, 2, 1)
    weights = [wg, wu, w_down, swap(wg), swap(wu), swap(w_down)]

    kv = hidden * (queries.shape[1] // HEAD_DIM) // (HEADS // KV_HEADS)
    key_block = lax.dynamic_slice_in_dim(key_rows, kv * HEAD_DIM, HEAD_DIM, 1)
    value_block = lax.dynamic_slice_in_dim(value_rows, kv * HEAD_DIM, HEAD_DIM, 1)
    mixed = attention(queries, key_block, value_block)
    proj = out_proj.reshape(out_proj.shape[0], 8, COLS)
    part = jnp.einsum("tk,khc->htc", mixed, proj, preferred_element_type=f32).astype(bf16)
    attn = lax.psum_scatter(part, "hidden", scatter_dimension=0, tiled=True)[0]

    route_slot = after(route_slot, part)
    slot_ids = jnp.arange(FETCH, dtype=jnp.int32)
    chosen = route_slot[:, :, None] == slot_ids[None, None, :]
    slot_weight = jnp.sum(jnp.where(chosen, route_weight[:, :, None], 0.0), axis=1)
    used = jnp.any(chosen, axis=1)
    lower = (
        lax.broadcasted_iota(jnp.int32, (tokens, tokens), 0)
        >= lax.broadcasted_iota(jnp.int32, (tokens, tokens), 1)
    ).astype(bf16)
    position = mm(lower, used.astype(bf16), NN).astype(jnp.int32) - 1
    position = jnp.where(used, position, -1)
    pos_t, weight_t = position.T, slot_weight.T

    def one_hot(start, size):
        caps = start + jnp.arange(size, dtype=jnp.int32)
        hit = pos_t[:, None, :] == caps[None, :, None]
        weight = jnp.sum(jnp.where(hit, weight_t[:, None, :], 0.0), axis=2)
        return hit.astype(bf16).reshape(FETCH * size, tokens), weight.reshape(-1, 1)

    cot_half = lax.dynamic_slice_in_dim(cotangent, core * HALF, HALF, 1)

    def grad_rows(start, size):
        pick, weight = one_hot(start, size)
        return (mm(pick, cot_half, NN) * weight).astype(bf16).reshape(FETCH, size, HALF)

    pick, row_weight = one_hot(0, CAP)
    g_first = exchange(after(grad_rows(0, SPLIT[0]), pick, row_weight))
    g_first_oth = swap(g_first)

    first_col = hidden * COLS
    res_share = lax.dynamic_slice_in_dim(residual, first_col, COLS, 1)
    gain = lax.dynamic_slice_in_dim(norm_gain, first_col, COLS, 0)
    stream = res_share.astype(f32) + attn.astype(f32)
    square = lax.psum(jnp.sum(stream * stream, axis=1), "hidden") / D
    normed = (stream * lax.rsqrt(square + epsilon)[:, None] * gain[None, :]).astype(bf16)

    x_part = mm(pick, normed, NN).astype(bf16).reshape(FETCH, CAP, COLS)
    x_part = exchange(after(x_part, g_first, *weights))
    x_rows = lax.all_gather(x_part, "hidden", axis=0, tiled=False)
    g_second = exchange(after(grad_rows(SPLIT[0], SPLIT[1]), x_part, g_first_oth))
    g_parts = [g_first, g_first_oth, g_second, swap(g_second)]

    own_col = lax.dynamic_slice_in_dim(fetch_list, group, 1, 1)[:, 0]
    experts = own_col - group * EXP_GROUP
    scalars = (*rows_order(experts), core_arr)
    tables = grad_order(experts)
    high = row_weight.astype(bf16)
    low = (row_weight - high.astype(f32)).astype(bf16)
    x_rows, high, low, *tables = lax.optimization_barrier((x_rows, high, low, *tables))
    out_rows, act, dgu, d_half = rows_call(scalars, x_rows, g_parts, weights)

    out_share = lax.psum_scatter(out_rows, "hidden", scatter_dimension=0, tiled=True)[0]
    d_back = exchange(d_half)
    grad_gate, grad_up, grad_down = grads_call(
        *tables, core_arr, x_rows, g_parts, after(act, d_back), dgu
    )
    out_back = exchange(after(out_share, d_back))

    d_tok = mm(pick, d_back.reshape(-1, HALF), TN).astype(bf16)
    d_tok = d_tok.reshape(tokens, 4, COLS).transpose(1, 0, 2)
    grad_normed = lax.psum_scatter(
        d_tok, "hidden", scatter_dimension=0, tiled=True, axis_index_groups=Z_GROUPS
    )[0]

    out_back = out_back.reshape(-1, COLS)
    moe = mm(pick * high, out_back, TN) + mm(pick * low, out_back, TN)
    layer_out = (stream + moe).astype(bf16)
    return (
        layer_out,
        grad_normed,
        grad_gate.transpose(0, 2, 1),
        grad_up.transpose(0, 2, 1),
        grad_down,
    )


def solution(mesh):
    return jax.shard_map(
        shards,
        mesh=mesh,
        in_specs=(
            P("group", "hidden"),
            P("group", None),
            P("group", None),
            P("hidden", None),
            P("group", None),
            P(),
            P("group", None, "hidden"),
            P("group", None, "hidden"),
            P("group", "hidden", None),
            P("group", None),
            P("group", None),
            P(),
            P("group", None),
        ),
        out_specs=(
            P("group", "hidden"),
            P("group", "hidden"),
            P("group", None, "hidden"),
            P("group", None, "hidden"),
            P("group", "hidden", None),
        ),
        check_vma=False,
    )
```

```python
import math

import jax
import jax.numpy as jnp
from jax import lax
from jax.experimental import pallas as pl
from jax.experimental.pallas import tpu as pltpu
from jax.sharding import PartitionSpec as P

D = 2048
HEADS = 32
KV_HEADS = 4
HEAD_DIM = 128
EXP_GROUP = 8
FETCH = 16
CAP = 240
UNITS = 96
PAD = 128
COLS = 256
HALF = 1024
STEPS = FETCH + EXP_GROUP
SPLIT = (80, 160)

epsilon = 1e-06
bf16 = jnp.bfloat16
f32 = jnp.float32

NT = (((1,), (1,)), ((), ()))
NN = (((1,), (0,)), ((), ()))
TN = (((0,), (0,)), ((), ()))


def mm(a, b, dims):
    return lax.dot_general(a, b, dims, preferred_element_type=f32)


def attention(queries, key_block, value_block):
    tokens = queries.shape[0]
    heads = queries.shape[1] // HEAD_DIM
    query = queries.reshape(tokens, heads, HEAD_DIM)
    scores = jnp.einsum("thd,sd->hts", query, key_block, preferred_element_type=f32)
    scores = scores / math.sqrt(HEAD_DIM)
    row_pos = lax.broadcasted_iota(jnp.int32, (tokens, tokens), 0)
    col_pos = lax.broadcasted_iota(jnp.int32, (tokens, tokens), 1)
    scores = jnp.where(row_pos >= col_pos, scores, -1e30)
    weights = jnp.exp(scores - jnp.max(scores, axis=-1, keepdims=True))
    probs = (weights / jnp.sum(weights, axis=-1, keepdims=True)).astype(bf16)
    mixed = jnp.einsum("hts,sd->thd", probs, value_block, preferred_element_type=f32)
    return mixed.astype(bf16).reshape(tokens, heads * HEAD_DIM)


def rows_kernel(order_ref, expert_ref, fresh_ref, core_ref, x_ref, *refs):
    g_refs = refs[: 2 * len(SPLIT)]
    (
        wg_ref, wu_ref, wd_ref, wg_oth_ref, wu_oth_ref, wd_oth_ref,
        out_ref, act_ref, dgu_ref, d_ref, wgu, wdp,
    ) = refs[2 * len(SPLIT) :]
    step = pl.program_id(0)
    core = core_ref[0]

    @pl.when(step == 0)
    def _():
        for ref in (wgu, wdp):
            for start in range(0, ref.shape[0], PAD):
                ref[start + UNITS : start + PAD, :] = jnp.zeros((PAD - UNITS, D), bf16)

    @pl.when(fresh_ref[step] == 1)
    def _():
        for i, ref in enumerate((wg_ref, wu_ref, wg_oth_ref, wu_oth_ref)):
            wgu[i * PAD : i * PAD + UNITS, :] = ref[0]
        own = pl.ds(pl.multiple_of(core * HALF, HALF), HALF)
        oth = pl.ds(pl.multiple_of(HALF - core * HALF, HALF), HALF)
        for i, ref in enumerate((wd_ref, wd_oth_ref)):
            wdp[i * PAD : i * PAD + UNITS, :HALF] = ref[0, :, own]
            wdp[i * PAD : i * PAD + UNITS, HALF:] = ref[0, :, oth]

    x = jnp.concatenate([x_ref[block, 0] for block in range(D // COLS)], axis=1)
    pre = mm(x, wgu[...], NT)
    g = jnp.concatenate(
        [
            jnp.concatenate([g_refs[2 * i][0], g_refs[2 * i + 1][0]], axis=1)
            for i in range(len(SPLIT))
        ],
        axis=0,
    )
    d_act = mm(g, wdp[...], NT)
    hidden = []
    for i in range(2):
        gate = pre[:, 2 * i * PAD : (2 * i + 1) * PAD]
        up = pre[:, (2 * i + 1) * PAD : (2 * i + 2) * PAD]
        d_part = d_act[:, i * PAD : (i + 1) * PAD]
        sig = jax.nn.sigmoid(gate)
        swish = gate * sig
        if i == 0:
            act = (swish * up).astype(bf16)
        hidden.append((d_part * up * sig * (1.0 + gate * (1.0 - sig))).astype(bf16))
        hidden.append((d_part * swish).astype(bf16))
    act_ref[0] = act
    dgu_ref[0, :, :PAD] = hidden[0]
    dgu_ref[0, :, PAD:] = hidden[1]
    for half, base in enumerate((core * 4, 4 - core * 4)):
        for block in range(4):
            col = half * HALF + block * COLS
            out_ref[base + block, 0] = mm(act, wdp[:PAD, col : col + COLS], NN).astype(bf16)
    both = jnp.concatenate(hidden, axis=1)
    for block in range(4):
        col = pl.ds(pl.multiple_of((2 * block + core) * COLS, COLS), COLS)
        d_ref[0, :, block * COLS : (block + 1) * COLS] = mm(both, wgu[:, col], NN).astype(bf16)


def rows_call(scalars, x_rows, g_parts, weights):
    weight = pl.BlockSpec((1, UNITS, D), lambda i, o, e, n, c: (e[i], 0, 0))
    cols8 = pl.BlockSpec((8, 1, CAP, COLS), lambda i, o, e, n, c: (0, o[i], 0, 0))

    def flat(size, width):
        return pl.BlockSpec((1, size, width), lambda i, o, e, n, c: (o[i], 0, 0))

    halves = [flat(size, HALF) for size in SPLIT for _ in range(2)]
    return pl.pallas_call(
        rows_kernel,
        grid_spec=pltpu.PrefetchScalarGridSpec(
            num_scalar_prefetch=4,
            grid=(FETCH,),
            in_specs=[cols8, *halves, *[weight] * 6],
            out_specs=[cols8, flat(CAP, PAD), flat(CAP, 2 * PAD), flat(CAP, HALF)],
            scratch_shapes=[pltpu.VMEM((4 * PAD, D), bf16), pltpu.VMEM((2 * PAD, D), bf16)],
        ),
        out_shape=[
            jax.ShapeDtypeStruct((8, FETCH, CAP, COLS), bf16),
            jax.ShapeDtypeStruct((FETCH, CAP, PAD), bf16),
            jax.ShapeDtypeStruct((FETCH, CAP, 2 * PAD), bf16),
            jax.ShapeDtypeStruct((FETCH, CAP, HALF), bf16),
        ],
        compiler_params=pltpu.CompilerParams(vmem_limit_bytes=56 << 20),
        cost_estimate=pl.CostEstimate(
            flops=2 * 9 * FETCH * CAP * D * PAD, bytes_accessed=80 << 20, transcendentals=0
        ),
        name="expert_rows",
    )(*scalars, x_rows, *g_parts, *weights)


def grads_kernel(chunk_ref, expert_ref, real_ref, last_ref, core_ref, x_ref, *refs):
    g_refs = refs[: 2 * len(SPLIT)]
    act_ref, dgu_ref, gg_ref, gu_ref, gd_ref, acc_gu, acc_d = refs[2 * len(SPLIT) :]
    step = pl.program_id(0)
    core = core_ref[0]
    kind, last = real_ref[step], last_ref[step]

    def chunk(first):
        d_gu, act = dgu_ref[0].T, act_ref[0].T
        for block in range(D // COLS):
            place = slice(block * COLS, (block + 1) * COLS)
            part = mm(d_gu, x_ref[block, 0], NN)
            acc_gu[:, place] = part if first else acc_gu[:, place] + part
        for half in range(2):
            for block in range(HALF // COLS):
                place = slice(block * COLS, (block + 1) * COLS)
                g = jnp.concatenate(
                    [g_refs[2 * i + half][0, :, place] for i in range(len(SPLIT))], axis=0
                )
                into = slice(half * HALF + block * COLS, half * HALF + (block + 1) * COLS)
                part = mm(act, g, NN)
                acc_d[:, into] = part if first else acc_d[:, into] + part

    @pl.when(kind == 1)
    def _():
        chunk(True)

    @pl.when(kind == 2)
    def _():
        chunk(False)

    @pl.when((last == 1) & (kind == 0))
    def _():
        for ref in (gg_ref, gu_ref, gd_ref):
            ref[...] = jnp.zeros_like(ref)

    @pl.when((last == 1) & (kind != 0))
    def _():
        gg_ref[0] = acc_gu[:UNITS, :].astype(bf16)
        gu_ref[0] = acc_gu[PAD : PAD + UNITS, :].astype(bf16)
        for half, base in enumerate((core * HALF, HALF - core * HALF)):
            col = pl.ds(pl.multiple_of(base, HALF), HALF)
            gd_ref[0, :, col] = acc_d[:UNITS, half * HALF : (half + 1) * HALF].astype(bf16)


def grads_call(chunk, expert, real, last, core, x_rows, g_parts, act, dgu):
    weight = pl.BlockSpec((1, UNITS, D), lambda i, k, e, r, l, c: (e[i], 0, 0))

    def flat(size, width):
        return pl.BlockSpec((1, size, width), lambda i, k, e, r, l, c: (k[i], 0, 0))

    halves = [flat(size, HALF) for size in SPLIT for _ in range(2)]
    return pl.pallas_call(
        grads_kernel,
        grid_spec=pltpu.PrefetchScalarGridSpec(
            num_scalar_prefetch=5,
            grid=(STEPS,),
            in_specs=[
                pl.BlockSpec((8, 1, CAP, COLS), lambda i, k, e, r, l, c: (0, k[i], 0, 0)),
                *halves,
                flat(CAP, PAD),
                flat(CAP, 2 * PAD),
            ],
            out_specs=[weight, weight, weight],
            scratch_shapes=[pltpu.VMEM((2 * PAD, D), f32), pltpu.VMEM((PAD, D), f32)],
        ),
        out_shape=[jax.ShapeDtypeStruct((EXP_GROUP, UNITS, D), bf16)] * 3,
        compiler_params=pltpu.CompilerParams(vmem_limit_bytes=56 << 20),
        cost_estimate=pl.CostEstimate(
            flops=2 * 3 * FETCH * CAP * D * PAD, bytes_accessed=45 << 20, transcendentals=0
        ),
        name="weight_grads",
    )(chunk, expert, real, last, core, x_rows, *g_parts, act, dgu)


def grad_order(experts):
    ids = jnp.arange(FETCH, dtype=jnp.int32)
    own = jnp.arange(EXP_GROUP, dtype=jnp.int32)
    listed = experts[None, :] == own[:, None]
    first = jnp.min(jnp.where(listed, ids[None, :], FETCH), axis=1)
    first = jnp.where(first == FETCH, 0, first)
    key = jnp.concatenate([own * 32, experts * 32 + 1 + ids])
    chunk = jnp.concatenate([first, ids])
    owner = jnp.concatenate([own, experts])
    rank = jnp.sum((key[None, :] < key[:, None]).astype(jnp.int32), axis=1)
    place = rank[:, None] == jnp.arange(STEPS, dtype=jnp.int32)[None, :]

    def ordered(values):
        return jnp.sum(jnp.where(place, values[:, None], 0), axis=0)

    count = jnp.sum((owner[None, :] == owner[:, None]) & (key[None, :] > key[:, None]), axis=1)
    earlier = (experts[None, :] == experts[:, None]) & (ids[None, :] < ids[:, None])
    again = jnp.any(earlier, axis=1).astype(jnp.int32)
    real = jnp.concatenate([jnp.zeros((EXP_GROUP,), jnp.int32), 1 + again])
    last = (count == 0).astype(jnp.int32)
    return ordered(chunk), ordered(owner), ordered(real), ordered(last)


def rows_order(experts):
    ids = jnp.arange(FETCH, dtype=jnp.int32)
    key = experts * FETCH + ids
    rank = jnp.sum((key[None, :] < key[:, None]).astype(jnp.int32), axis=1)
    place = rank[:, None] == ids[None, :]
    order = jnp.sum(jnp.where(place, ids[:, None], 0), axis=0)
    expert = jnp.sum(jnp.where(place, experts[:, None], 0), axis=0)
    earlier = (experts[None, :] == experts[:, None]) & (ids[None, :] < ids[:, None])
    new = 1 - jnp.any(earlier, axis=1).astype(jnp.int32)
    fresh = jnp.sum(jnp.where(place, new[:, None], 0), axis=0)
    return order, expert, fresh


Z_GROUPS = [[0, 2, 4, 6], [1, 3, 5, 7]]
PAIRS = [(i, i ^ 1) for i in range(8)]


def after(value, *others):
    return lax.optimization_barrier((value,) + others)[0]


def exchange(value, axis="group"):
    return lax.all_to_all(value, axis, split_axis=0, concat_axis=0, tiled=True)


def swap(value):
    return lax.ppermute(value, "hidden", PAIRS)


def shards(
    queries, key_rows, value_rows, out_proj, residual, norm_gain, w_gate, w_up, w_down,
    route_slot, route_weight, fetch_list, cotangent,
):
    tokens = queries.shape[0]
    hidden = lax.axis_index("hidden")
    group = lax.axis_index("group")
    core = hidden % 2
    core_arr = core.reshape(1).astype(jnp.int32)
    wg, wu = w_gate.transpose(0, 2, 1), w_up.transpose(0, 2, 1)
    weights = [wg, wu, w_down, swap(wg), swap(wu), swap(w_down)]

    kv = hidden * (queries.shape[1] // HEAD_DIM) // (HEADS // KV_HEADS)
    key_block = lax.dynamic_slice_in_dim(key_rows, kv * HEAD_DIM, HEAD_DIM, 1)
    value_block = lax.dynamic_slice_in_dim(value_rows, kv * HEAD_DIM, HEAD_DIM, 1)
    mixed = attention(queries, key_block, value_block)
    proj = out_proj.reshape(out_proj.shape[0], 8, COLS)
    part = jnp.einsum("tk,khc->htc", mixed, proj, preferred_element_type=f32).astype(bf16)
    attn = lax.psum_scatter(part, "hidden", scatter_dimension=0, tiled=True)[0]

    route_slot = after(route_slot, part)
    slot_ids = jnp.arange(FETCH, dtype=jnp.int32)
    chosen = route_slot[:, :, None] == slot_ids[None, None, :]
    slot_weight = jnp.sum(jnp.where(chosen, route_weight[:, :, None], 0.0), axis=1)
    used = jnp.any(chosen, axis=1)
    lower = (
        lax.broadcasted_iota(jnp.int32, (tokens, tokens), 0)
        >= lax.broadcasted_iota(jnp.int32, (tokens, tokens), 1)
    ).astype(bf16)
    position = mm(lower, used.astype(bf16), NN).astype(jnp.int32) - 1
    position = jnp.where(used, position, -1)
    pos_t, weight_t = position.T, slot_weight.T

    def one_hot(start, size):
        caps = start + jnp.arange(size, dtype=jnp.int32)
        hit = pos_t[:, None, :] == caps[None, :, None]
        weight = jnp.sum(jnp.where(hit, weight_t[:, None, :], 0.0), axis=2)
        return hit.astype(bf16).reshape(FETCH * size, tokens), weight.reshape(-1, 1)

    row_slot = lax.broadcasted_iota(jnp.int32, (FETCH, FETCH * CAP), 1) // CAP
    spread = (row_slot == lax.broadcasted_iota(jnp.int32, (FETCH, FETCH * CAP), 0)).astype(bf16)
    row_cap = lax.broadcasted_iota(jnp.int32, (tokens, FETCH * CAP), 1) % CAP
    hit_rows = mm(position.astype(bf16), spread, NN) == row_cap.astype(f32)
    high = slot_weight.astype(bf16)
    low = (slot_weight - high.astype(f32)).astype(bf16)
    into = hit_rows.astype(bf16)
    into_high = jnp.where(hit_rows, mm(high, spread, NN), 0.0).astype(bf16)
    into_low = jnp.where(hit_rows, mm(low, spread, NN), 0.0).astype(bf16)

    cot_half = lax.dynamic_slice_in_dim(cotangent, core * HALF, HALF, 1)

    def grad_rows(start, size):
        pick, weight = one_hot(start, size)
        return (mm(pick, cot_half, NN) * weight).astype(bf16).reshape(FETCH, size, HALF)

    pick, row_weight = one_hot(0, CAP)
    g_first = exchange(after(grad_rows(0, SPLIT[0]), pick, row_weight))
    g_first_oth = swap(g_first)

    second_rows = grad_rows(SPLIT[0], SPLIT[1])
    own_col = lax.dynamic_slice_in_dim(fetch_list, group, 1, 1)[:, 0]
    experts = own_col - group * EXP_GROUP
    scalars = (*rows_order(experts), core_arr)
    tables = grad_order(experts)
    attn, second_rows, scalars, tables, into, into_high, into_low = lax.optimization_barrier(
        (attn, second_rows, scalars, tables, into, into_high, into_low)
    )
    first_col = hidden * COLS
    res_share = lax.dynamic_slice_in_dim(residual, first_col, COLS, 1)
    gain = lax.dynamic_slice_in_dim(norm_gain, first_col, COLS, 0)
    stream = res_share.astype(f32) + attn.astype(f32)
    square = lax.psum(jnp.sum(stream * stream, axis=1), "hidden") / D
    normed = (stream * lax.rsqrt(square + epsilon)[:, None] * gain[None, :]).astype(bf16)

    x_part = mm(pick, normed, NN).astype(bf16).reshape(FETCH, CAP, COLS)
    x_part = exchange(after(x_part, g_first, *weights))
    x_rows = lax.all_gather(x_part, "hidden", axis=0, tiled=False)
    g_second = exchange(after(second_rows, x_part, g_first_oth))
    g_parts = [g_first, g_first_oth, g_second, swap(g_second)]

    out_rows, act, dgu, d_half = rows_call(scalars, x_rows, g_parts, weights)

    out_share = lax.psum_scatter(out_rows, "hidden", scatter_dimension=0, tiled=True)[0]
    d_back = exchange(d_half)
    grad_gate, grad_up, grad_down = grads_call(
        *tables, core_arr, x_rows, g_parts, after(act, d_back), dgu
    )
    out_back = exchange(after(out_share, d_back))

    d_tok = mm(into, d_back.reshape(-1, HALF), NN).astype(bf16)
    d_tok = d_tok.reshape(tokens, 4, COLS).transpose(1, 0, 2)
    grad_normed = lax.psum_scatter(
        d_tok, "hidden", scatter_dimension=0, tiled=True, axis_index_groups=Z_GROUPS
    )[0]

    out_back = out_back.reshape(-1, COLS)
    moe = mm(into_high, out_back, NN) + mm(into_low, out_back, NN)
    layer_out = (stream + moe).astype(bf16)
    return (
        layer_out,
        grad_normed,
        grad_gate.transpose(0, 2, 1),
        grad_up.transpose(0, 2, 1),
        grad_down,
    )


def solution(mesh):
    return jax.shard_map(
        shards,
        mesh=mesh,
        in_specs=(
            P("group", "hidden"),
            P("group", None),
            P("group", None),
            P("hidden", None),
            P("group", None),
            P(),
            P("group", None, "hidden"),
            P("group", None, "hidden"),
            P("group", "hidden", None),
            P("group", None),
            P("group", None),
            P(),
            P("group", None),
        ),
        out_specs=(
            P("group", "hidden"),
            P("group", "hidden"),
            P("group", None, "hidden"),
            P("group", None, "hidden"),
            P("group", "hidden", None),
        ),
        check_vma=False,
    )
```

```python
import math

import jax
import jax.numpy as jnp
from jax import lax
from jax.experimental import pallas as pl
from jax.experimental.pallas import tpu as pltpu
from jax.sharding import PartitionSpec as P

D = 2048
HEADS = 32
KV_HEADS = 4
HEAD_DIM = 128
EXP_GROUP = 8
FETCH = 16
CAP = 240
UNITS = 96
PAD = 128
COLS = 256
HALF = 1024
STEPS = FETCH + EXP_GROUP
SPLIT = (80, 160)

epsilon = 1e-06
bf16 = jnp.bfloat16
f32 = jnp.float32

NT = (((1,), (1,)), ((), ()))
NN = (((1,), (0,)), ((), ()))
TN = (((0,), (0,)), ((), ()))


def mm(a, b, dims):
    return lax.dot_general(a, b, dims, preferred_element_type=f32)


def attention(queries, key_block, value_block):
    tokens = queries.shape[0]
    heads = queries.shape[1] // HEAD_DIM
    query = queries.reshape(tokens, heads, HEAD_DIM)
    scores = jnp.einsum("thd,sd->hts", query, key_block, preferred_element_type=f32)
    scores = scores / math.sqrt(HEAD_DIM)
    row_pos = lax.broadcasted_iota(jnp.int32, (tokens, tokens), 0)
    col_pos = lax.broadcasted_iota(jnp.int32, (tokens, tokens), 1)
    scores = jnp.where(row_pos >= col_pos, scores, -1e30)
    weights = jnp.exp(scores - jnp.max(scores, axis=-1, keepdims=True))
    probs = (weights / jnp.sum(weights, axis=-1, keepdims=True)).astype(bf16)
    mixed = jnp.einsum("hts,sd->thd", probs, value_block, preferred_element_type=f32)
    return mixed.astype(bf16).reshape(tokens, heads * HEAD_DIM)


def rows_kernel(order_ref, expert_ref, fresh_ref, core_ref, x_ref, *refs):
    g_refs = refs[: 2 * len(SPLIT)]
    (
        wg_ref, wu_ref, wd_ref, wg_oth_ref, wu_oth_ref, wd_oth_ref,
        out_ref, act_ref, dgu_ref, d_ref, wgu, wdp,
    ) = refs[2 * len(SPLIT) :]
    step = pl.program_id(0)
    core = core_ref[0]

    @pl.when(step == 0)
    def _():
        for ref in (wgu, wdp):
            for start in range(0, ref.shape[0], PAD):
                ref[start + UNITS : start + PAD, :] = jnp.zeros((PAD - UNITS, D), bf16)

    @pl.when(fresh_ref[step] == 1)
    def _():
        for i, ref in enumerate((wg_ref, wu_ref, wg_oth_ref, wu_oth_ref)):
            wgu[i * PAD : i * PAD + UNITS, :] = ref[0]
        own = pl.ds(pl.multiple_of(core * HALF, HALF), HALF)
        oth = pl.ds(pl.multiple_of(HALF - core * HALF, HALF), HALF)
        for i, ref in enumerate((wd_ref, wd_oth_ref)):
            wdp[i * PAD : i * PAD + UNITS, :HALF] = ref[0, :, own]
            wdp[i * PAD : i * PAD + UNITS, HALF:] = ref[0, :, oth]

    x = jnp.concatenate([x_ref[block, 0] for block in range(D // COLS)], axis=1)
    pre = mm(x, wgu[...], NT)
    g = jnp.concatenate(
        [
            jnp.concatenate([g_refs[2 * i][0], g_refs[2 * i + 1][0]], axis=1)
            for i in range(len(SPLIT))
        ],
        axis=0,
    )
    d_act = mm(g, wdp[...], NT)
    hidden = []
    for i in range(2):
        gate = pre[:, 2 * i * PAD : (2 * i + 1) * PAD]
        up = pre[:, (2 * i + 1) * PAD : (2 * i + 2) * PAD]
        d_part = d_act[:, i * PAD : (i + 1) * PAD]
        sig = jax.nn.sigmoid(gate)
        swish = gate * sig
        if i == 0:
            act = (swish * up).astype(bf16)
        hidden.append((d_part * up * sig * (1.0 + gate * (1.0 - sig))).astype(bf16))
        hidden.append((d_part * swish).astype(bf16))
    act_ref[0] = act
    dgu_ref[0, :, :PAD] = hidden[0]
    dgu_ref[0, :, PAD:] = hidden[1]
    for half, base in enumerate((core * 4, 4 - core * 4)):
        for block in range(4):
            col = half * HALF + block * COLS
            out_ref[base + block, 0] = mm(act, wdp[:PAD, col : col + COLS], NN).astype(bf16)
    both = jnp.concatenate(hidden, axis=1)
    for block in range(4):
        col = pl.ds(pl.multiple_of((2 * block + core) * COLS, COLS), COLS)
        d_ref[0, :, block * COLS : (block + 1) * COLS] = mm(both, wgu[:, col], NN).astype(bf16)


def rows_call(scalars, x_rows, g_parts, weights):
    weight = pl.BlockSpec((1, UNITS, D), lambda i, o, e, n, c: (e[i], 0, 0))
    cols8 = pl.BlockSpec((8, 1, CAP, COLS), lambda i, o, e, n, c: (0, o[i], 0, 0))

    def flat(size, width):
        return pl.BlockSpec((1, size, width), lambda i, o, e, n, c: (o[i], 0, 0))

    halves = [flat(size, HALF) for size in SPLIT for _ in range(2)]
    return pl.pallas_call(
        rows_kernel,
        grid_spec=pltpu.PrefetchScalarGridSpec(
            num_scalar_prefetch=4,
            grid=(FETCH,),
            in_specs=[cols8, *halves, *[weight] * 6],
            out_specs=[cols8, flat(CAP, PAD), flat(CAP, 2 * PAD), flat(CAP, HALF)],
            scratch_shapes=[pltpu.VMEM((4 * PAD, D), bf16), pltpu.VMEM((2 * PAD, D), bf16)],
        ),
        out_shape=[
            jax.ShapeDtypeStruct((8, FETCH, CAP, COLS), bf16),
            jax.ShapeDtypeStruct((FETCH, CAP, PAD), bf16),
            jax.ShapeDtypeStruct((FETCH, CAP, 2 * PAD), bf16),
            jax.ShapeDtypeStruct((FETCH, CAP, HALF), bf16),
        ],
        compiler_params=pltpu.CompilerParams(vmem_limit_bytes=56 << 20),
        cost_estimate=pl.CostEstimate(
            flops=2 * 9 * FETCH * CAP * D * PAD, bytes_accessed=80 << 20, transcendentals=0
        ),
        name="expert_rows",
    )(*scalars, x_rows, *g_parts, *weights)


def grads_kernel(chunk_ref, expert_ref, real_ref, last_ref, core_ref, x_ref, *refs):
    g_refs = refs[: 2 * len(SPLIT)]
    act_ref, dgu_ref, gg_ref, gu_ref, gd_ref, acc_gu, acc_d = refs[2 * len(SPLIT) :]
    step = pl.program_id(0)
    core = core_ref[0]
    kind, last = real_ref[step], last_ref[step]

    def chunk(first):
        d_gu, act = dgu_ref[0].T, act_ref[0].T
        for block in range(D // COLS):
            place = slice(block * COLS, (block + 1) * COLS)
            part = mm(d_gu, x_ref[block, 0], NN)
            acc_gu[:, place] = part if first else acc_gu[:, place] + part
        for half in range(2):
            for block in range(HALF // COLS):
                place = slice(block * COLS, (block + 1) * COLS)
                g = jnp.concatenate(
                    [g_refs[2 * i + half][0, :, place] for i in range(len(SPLIT))], axis=0
                )
                into = slice(half * HALF + block * COLS, half * HALF + (block + 1) * COLS)
                part = mm(act, g, NN)
                acc_d[:, into] = part if first else acc_d[:, into] + part

    @pl.when(kind == 1)
    def _():
        chunk(True)

    @pl.when(kind == 2)
    def _():
        chunk(False)

    @pl.when((last == 1) & (kind == 0))
    def _():
        for ref in (gg_ref, gu_ref, gd_ref):
            ref[...] = jnp.zeros_like(ref)

    @pl.when((last == 1) & (kind != 0))
    def _():
        gg_ref[0] = acc_gu[:UNITS, :].astype(bf16)
        gu_ref[0] = acc_gu[PAD : PAD + UNITS, :].astype(bf16)
        for half, base in enumerate((core * HALF, HALF - core * HALF)):
            col = pl.ds(pl.multiple_of(base, HALF), HALF)
            gd_ref[0, :, col] = acc_d[:UNITS, half * HALF : (half + 1) * HALF].astype(bf16)


def grads_call(chunk, expert, real, last, core, x_rows, g_parts, act, dgu):
    weight = pl.BlockSpec((1, UNITS, D), lambda i, k, e, r, l, c: (e[i], 0, 0))

    def flat(size, width):
        return pl.BlockSpec((1, size, width), lambda i, k, e, r, l, c: (k[i], 0, 0))

    halves = [flat(size, HALF) for size in SPLIT for _ in range(2)]
    return pl.pallas_call(
        grads_kernel,
        grid_spec=pltpu.PrefetchScalarGridSpec(
            num_scalar_prefetch=5,
            grid=(STEPS,),
            in_specs=[
                pl.BlockSpec((8, 1, CAP, COLS), lambda i, k, e, r, l, c: (0, k[i], 0, 0)),
                *halves,
                flat(CAP, PAD),
                flat(CAP, 2 * PAD),
            ],
            out_specs=[weight, weight, weight],
            scratch_shapes=[pltpu.VMEM((2 * PAD, D), f32), pltpu.VMEM((PAD, D), f32)],
        ),
        out_shape=[jax.ShapeDtypeStruct((EXP_GROUP, UNITS, D), bf16)] * 3,
        compiler_params=pltpu.CompilerParams(vmem_limit_bytes=56 << 20),
        cost_estimate=pl.CostEstimate(
            flops=2 * 3 * FETCH * CAP * D * PAD, bytes_accessed=45 << 20, transcendentals=0
        ),
        name="weight_grads",
    )(chunk, expert, real, last, core, x_rows, *g_parts, act, dgu)


def grad_order(experts):
    ids = jnp.arange(FETCH, dtype=jnp.int32)
    own = jnp.arange(EXP_GROUP, dtype=jnp.int32)
    listed = experts[None, :] == own[:, None]
    first = jnp.min(jnp.where(listed, ids[None, :], FETCH), axis=1)
    first = jnp.where(first == FETCH, 0, first)
    key = jnp.concatenate([own * 32, experts * 32 + 1 + ids])
    chunk = jnp.concatenate([first, ids])
    owner = jnp.concatenate([own, experts])
    rank = jnp.sum((key[None, :] < key[:, None]).astype(jnp.int32), axis=1)
    place = rank[:, None] == jnp.arange(STEPS, dtype=jnp.int32)[None, :]

    def ordered(values):
        return jnp.sum(jnp.where(place, values[:, None], 0), axis=0)

    count = jnp.sum((owner[None, :] == owner[:, None]) & (key[None, :] > key[:, None]), axis=1)
    earlier = (experts[None, :] == experts[:, None]) & (ids[None, :] < ids[:, None])
    again = jnp.any(earlier, axis=1).astype(jnp.int32)
    real = jnp.concatenate([jnp.zeros((EXP_GROUP,), jnp.int32), 1 + again])
    last = (count == 0).astype(jnp.int32)
    return ordered(chunk), ordered(owner), ordered(real), ordered(last)


def rows_order(experts):
    ids = jnp.arange(FETCH, dtype=jnp.int32)
    key = experts * FETCH + ids
    rank = jnp.sum((key[None, :] < key[:, None]).astype(jnp.int32), axis=1)
    place = rank[:, None] == ids[None, :]
    order = jnp.sum(jnp.where(place, ids[:, None], 0), axis=0)
    expert = jnp.sum(jnp.where(place, experts[:, None], 0), axis=0)
    earlier = (experts[None, :] == experts[:, None]) & (ids[None, :] < ids[:, None])
    new = 1 - jnp.any(earlier, axis=1).astype(jnp.int32)
    fresh = jnp.sum(jnp.where(place, new[:, None], 0), axis=0)
    return order, expert, fresh


Z_GROUPS = [[0, 2, 4, 6], [1, 3, 5, 7]]
PAIRS = [(i, i ^ 1) for i in range(8)]


def after(value, *others):
    return lax.optimization_barrier((value,) + others)[0]


def exchange(value, axis="group"):
    return lax.all_to_all(value, axis, split_axis=0, concat_axis=0, tiled=True)


def swap(value):
    return lax.ppermute(value, "hidden", PAIRS)


def shards(
    queries, key_rows, value_rows, out_proj, residual, norm_gain, w_gate, w_up, w_down,
    route_slot, route_weight, fetch_list, cotangent,
):
    tokens = queries.shape[0]
    hidden = lax.axis_index("hidden")
    group = lax.axis_index("group")
    core = hidden % 2
    core_arr = core.reshape(1).astype(jnp.int32)
    wg, wu = w_gate.transpose(0, 2, 1), w_up.transpose(0, 2, 1)
    weights = [wg, wu, w_down, swap(wg), swap(wu), swap(w_down)]

    kv = hidden * (queries.shape[1] // HEAD_DIM) // (HEADS // KV_HEADS)
    key_block = lax.dynamic_slice_in_dim(key_rows, kv * HEAD_DIM, HEAD_DIM, 1)
    value_block = lax.dynamic_slice_in_dim(value_rows, kv * HEAD_DIM, HEAD_DIM, 1)
    mixed = attention(queries, key_block, value_block)
    proj = out_proj.reshape(out_proj.shape[0], 8, COLS)
    part = jnp.einsum("tk,khc->htc", mixed, proj, preferred_element_type=f32).astype(bf16)
    attn = lax.psum_scatter(part, "hidden", scatter_dimension=0, tiled=True)[0]

    route_slot = after(route_slot, part)
    slot_ids = jnp.arange(FETCH, dtype=jnp.int32)
    chosen = route_slot[:, :, None] == slot_ids[None, None, :]
    slot_weight = jnp.sum(jnp.where(chosen, route_weight[:, :, None], 0.0), axis=1)
    used = jnp.any(chosen, axis=1)
    lower = (
        lax.broadcasted_iota(jnp.int32, (tokens, tokens), 0)
        >= lax.broadcasted_iota(jnp.int32, (tokens, tokens), 1)
    ).astype(bf16)
    position = mm(lower, used.astype(bf16), NN).astype(jnp.int32) - 1
    position = jnp.where(used, position, -1)
    pos_t, weight_t = position.T, slot_weight.T

    def one_hot(start, size):
        caps = start + jnp.arange(size, dtype=jnp.int32)
        hit = pos_t[:, None, :] == caps[None, :, None]
        weight = jnp.sum(jnp.where(hit, weight_t[:, None, :], 0.0), axis=2)
        return hit.astype(bf16).reshape(FETCH * size, tokens), weight.reshape(-1, 1)

    row_slot = lax.broadcasted_iota(jnp.int32, (FETCH, FETCH * CAP), 1) // CAP
    spread = (row_slot == lax.broadcasted_iota(jnp.int32, (FETCH, FETCH * CAP), 0)).astype(bf16)
    row_cap = lax.broadcasted_iota(jnp.int32, (tokens, FETCH * CAP), 1) % CAP
    hit_rows = mm(position.astype(bf16), spread, NN) == row_cap.astype(f32)
    high = slot_weight.astype(bf16)
    low = (slot_weight - high.astype(f32)).astype(bf16)
    into = hit_rows.astype(bf16)
    into_high = jnp.where(hit_rows, mm(high, spread, NN), 0.0).astype(bf16)
    into_low = jnp.where(hit_rows, mm(low, spread, NN), 0.0).astype(bf16)

    cot_half = lax.dynamic_slice_in_dim(cotangent, core * HALF, HALF, 1)

    def grad_rows(start, size):
        pick, weight = one_hot(start, size)
        return (mm(pick, cot_half, NN) * weight).astype(bf16).reshape(FETCH, size, HALF)

    pick, row_weight = one_hot(0, CAP)
    g_first = exchange(after(grad_rows(0, SPLIT[0]), pick, row_weight))

    second_rows = grad_rows(SPLIT[0], SPLIT[1])
    own_col = lax.dynamic_slice_in_dim(fetch_list, group, 1, 1)[:, 0]
    experts = own_col - group * EXP_GROUP
    scalars = (*rows_order(experts), core_arr)
    tables = grad_order(experts)
    attn, second_rows, scalars, tables, into, into_high, into_low, weights = (
        lax.optimization_barrier(
            (attn, second_rows, scalars, tables, into, into_high, into_low, weights)
        )
    )
    first_col = hidden * COLS
    res_share = lax.dynamic_slice_in_dim(residual, first_col, COLS, 1)
    gain = lax.dynamic_slice_in_dim(norm_gain, first_col, COLS, 0)
    stream = res_share.astype(f32) + attn.astype(f32)
    own_square = jnp.sum(stream * stream, axis=1)
    square = own_square
    for turn in range(1, 8):
        square = square + lax.ppermute(own_square, "hidden", [(i, i ^ turn) for i in range(8)])
    square = square / D
    normed = (stream * lax.rsqrt(square + epsilon)[:, None] * gain[None, :]).astype(bf16)

    x_part = mm(pick, normed, NN).astype(bf16).reshape(FETCH, CAP, COLS)
    x_part = exchange(after(x_part, g_first))
    x_rows = lax.all_gather(x_part, "hidden", axis=0, tiled=False)
    g_second = exchange(after(second_rows, x_part))
    g_parts = [g_first, swap(after(g_first, g_second)), g_second, swap(g_second)]

    out_rows, act, dgu, d_half = rows_call(scalars, x_rows, g_parts, weights)

    out_share = lax.psum_scatter(out_rows, "hidden", scatter_dimension=0, tiled=True)[0]
    d_back = exchange(d_half)
    grad_gate, grad_up, grad_down = grads_call(
        *tables, core_arr, x_rows, g_parts, after(act, d_back), dgu
    )
    out_back = exchange(after(out_share, d_back))

    d_tok = mm(into, d_back.reshape(-1, HALF), NN).astype(bf16)
    d_tok = d_tok.reshape(tokens, 4, COLS).transpose(1, 0, 2)
    grad_normed = lax.psum_scatter(
        d_tok, "hidden", scatter_dimension=0, tiled=True, axis_index_groups=Z_GROUPS
    )[0]

    out_back = out_back.reshape(-1, COLS)
    moe = mm(into_high, out_back, NN) + mm(into_low, out_back, NN)
    layer_out = (stream + moe).astype(bf16)
    return (
        layer_out,
        grad_normed,
        grad_gate.transpose(0, 2, 1),
        grad_up.transpose(0, 2, 1),
        grad_down,
    )


def solution(mesh):
    return jax.shard_map(
        shards,
        mesh=mesh,
        in_specs=(
            P("group", "hidden"),
            P("group", None),
            P("group", None),
            P("hidden", None),
            P("group", None),
            P(),
            P("group", None, "hidden"),
            P("group", None, "hidden"),
            P("group", "hidden", None),
            P("group", None),
            P("group", None),
            P(),
            P("group", None),
        ),
        out_specs=(
            P("group", "hidden"),
            P("group", "hidden"),
            P("group", None, "hidden"),
            P("group", None, "hidden"),
            P("group", "hidden", None),
        ),
        check_vma=False,
    )
```

```python
import math

import jax
import jax.numpy as jnp
from jax import lax
from jax.experimental import pallas as pl
from jax.experimental.pallas import tpu as pltpu
from jax.sharding import PartitionSpec as P

D = 2048
HEADS = 32
KV_HEADS = 4
HEAD_DIM = 128
EXP_GROUP = 8
FETCH = 16
CAP = 240
UNITS = 96
PAD = 128
COLS = 256
HALF = 1024
STEPS = FETCH + EXP_GROUP
SPLIT = (80, 160)

epsilon = 1e-06
bf16 = jnp.bfloat16
f32 = jnp.float32

NT = (((1,), (1,)), ((), ()))
NN = (((1,), (0,)), ((), ()))
TN = (((0,), (0,)), ((), ()))


def mm(a, b, dims):
    return lax.dot_general(a, b, dims, preferred_element_type=f32)


def attention(queries, key_block, value_block):
    tokens = queries.shape[0]
    heads = queries.shape[1] // HEAD_DIM
    query = queries.reshape(tokens, heads, HEAD_DIM)
    scores = jnp.einsum("thd,sd->hts", query, key_block, preferred_element_type=f32)
    scores = scores / math.sqrt(HEAD_DIM)
    row_pos = lax.broadcasted_iota(jnp.int32, (tokens, tokens), 0)
    col_pos = lax.broadcasted_iota(jnp.int32, (tokens, tokens), 1)
    scores = jnp.where(row_pos >= col_pos, scores, -1e30)
    weights = jnp.exp(scores - jnp.max(scores, axis=-1, keepdims=True))
    probs = (weights / jnp.sum(weights, axis=-1, keepdims=True)).astype(bf16)
    mixed = jnp.einsum("hts,sd->thd", probs, value_block, preferred_element_type=f32)
    return mixed.astype(bf16).reshape(tokens, heads * HEAD_DIM)


def rows_kernel(order_ref, expert_ref, fresh_ref, core_ref, x_ref, *refs):
    g_refs = refs[: 2 * len(SPLIT)]
    (
        wg_ref, wu_ref, wd_ref, wg_oth_ref, wu_oth_ref, wd_oth_ref,
        out_ref, act_ref, dgu_ref, d_ref, wgu, wdp,
    ) = refs[2 * len(SPLIT) :]
    step = pl.program_id(0)
    core = core_ref[0]

    @pl.when(step == 0)
    def _():
        for ref in (wgu, wdp):
            for start in range(0, ref.shape[0], PAD):
                ref[start + UNITS : start + PAD, :] = jnp.zeros((PAD - UNITS, D), bf16)

    @pl.when(fresh_ref[step] == 1)
    def _():
        for i, ref in enumerate((wg_ref, wu_ref, wg_oth_ref, wu_oth_ref)):
            wgu[i * PAD : i * PAD + UNITS, :] = ref[0]
        own = pl.ds(pl.multiple_of(core * HALF, HALF), HALF)
        oth = pl.ds(pl.multiple_of(HALF - core * HALF, HALF), HALF)
        for i, ref in enumerate((wd_ref, wd_oth_ref)):
            wdp[i * PAD : i * PAD + UNITS, :HALF] = ref[0, :, own]
            wdp[i * PAD : i * PAD + UNITS, HALF:] = ref[0, :, oth]

    x = jnp.concatenate([x_ref[block, 0] for block in range(D // COLS)], axis=1)
    pre = mm(x, wgu[...], NT)
    g = jnp.concatenate(
        [
            jnp.concatenate([g_refs[2 * i][0], g_refs[2 * i + 1][0]], axis=1)
            for i in range(len(SPLIT))
        ],
        axis=0,
    )
    d_act = mm(g, wdp[...], NT)
    acts, hidden = [], []
    for i in range(2):
        gate = pre[:, 2 * i * PAD : (2 * i + 1) * PAD]
        up = pre[:, (2 * i + 1) * PAD : (2 * i + 2) * PAD]
        d_part = d_act[:, i * PAD : (i + 1) * PAD]
        sig = jax.nn.sigmoid(gate)
        swish = gate * sig
        acts.append((swish * up).astype(bf16))
        hidden.append((d_part * up * sig * (1.0 + gate * (1.0 - sig))).astype(bf16))
        hidden.append((d_part * swish).astype(bf16))
    act_ref[0] = acts[0]
    dgu_ref[0, :, :PAD] = hidden[0]
    dgu_ref[0, :, PAD:] = hidden[1]
    act = jnp.concatenate(acts, axis=1)
    for block in range(4):
        half = core if block < 2 else 1 - core
        col = half * HALF + (2 * (block % 2) + core) * COLS
        col = pl.ds(pl.multiple_of(col, COLS), COLS)
        out_ref[block, 0] = mm(act, wdp[:, col], NN).astype(bf16)
    both = jnp.concatenate(hidden, axis=1)
    for block in range(4):
        col = pl.ds(pl.multiple_of((2 * block + core) * COLS, COLS), COLS)
        d_ref[0, :, block * COLS : (block + 1) * COLS] = mm(both, wgu[:, col], NN).astype(bf16)


def rows_call(scalars, x_rows, g_parts, weights):
    weight = pl.BlockSpec((1, UNITS, D), lambda i, o, e, n, c: (e[i], 0, 0))
    cols8 = pl.BlockSpec((8, 1, CAP, COLS), lambda i, o, e, n, c: (0, o[i], 0, 0))

    def flat(size, width):
        return pl.BlockSpec((1, size, width), lambda i, o, e, n, c: (o[i], 0, 0))

    halves = [flat(size, HALF) for size in SPLIT for _ in range(2)]
    return pl.pallas_call(
        rows_kernel,
        grid_spec=pltpu.PrefetchScalarGridSpec(
            num_scalar_prefetch=4,
            grid=(FETCH,),
            in_specs=[cols8, *halves, *[weight] * 6],
            out_specs=[
                pl.BlockSpec((4, 1, CAP, COLS), lambda i, o, e, n, c: (0, o[i], 0, 0)),
                flat(CAP, PAD),
                flat(CAP, 2 * PAD),
                flat(CAP, HALF),
            ],
            scratch_shapes=[pltpu.VMEM((4 * PAD, D), bf16), pltpu.VMEM((2 * PAD, D), bf16)],
        ),
        out_shape=[
            jax.ShapeDtypeStruct((4, FETCH, CAP, COLS), bf16),
            jax.ShapeDtypeStruct((FETCH, CAP, PAD), bf16),
            jax.ShapeDtypeStruct((FETCH, CAP, 2 * PAD), bf16),
            jax.ShapeDtypeStruct((FETCH, CAP, HALF), bf16),
        ],
        compiler_params=pltpu.CompilerParams(vmem_limit_bytes=56 << 20),
        cost_estimate=pl.CostEstimate(
            flops=2 * 9 * FETCH * CAP * D * PAD, bytes_accessed=80 << 20, transcendentals=0
        ),
        name="expert_rows",
    )(*scalars, x_rows, *g_parts, *weights)


def grads_kernel(chunk_ref, expert_ref, real_ref, last_ref, core_ref, x_ref, *refs):
    g_refs = refs[: 2 * len(SPLIT)]
    act_ref, dgu_ref, gg_ref, gu_ref, gd_ref, acc_gu, acc_d = refs[2 * len(SPLIT) :]
    step = pl.program_id(0)
    core = core_ref[0]
    kind, last = real_ref[step], last_ref[step]

    def chunk(first):
        d_gu, act = dgu_ref[0].T, act_ref[0].T
        for block in range(D // COLS):
            place = slice(block * COLS, (block + 1) * COLS)
            part = mm(d_gu, x_ref[block, 0], NN)
            acc_gu[:, place] = part if first else acc_gu[:, place] + part
        for half in range(2):
            for block in range(HALF // COLS):
                place = slice(block * COLS, (block + 1) * COLS)
                g = jnp.concatenate(
                    [g_refs[2 * i + half][0, :, place] for i in range(len(SPLIT))], axis=0
                )
                into = slice(half * HALF + block * COLS, half * HALF + (block + 1) * COLS)
                part = mm(act, g, NN)
                acc_d[:, into] = part if first else acc_d[:, into] + part

    @pl.when(kind == 1)
    def _():
        chunk(True)

    @pl.when(kind == 2)
    def _():
        chunk(False)

    @pl.when((last == 1) & (kind == 0))
    def _():
        for ref in (gg_ref, gu_ref, gd_ref):
            ref[...] = jnp.zeros_like(ref)

    @pl.when((last == 1) & (kind != 0))
    def _():
        gg_ref[0] = acc_gu[:UNITS, :].astype(bf16)
        gu_ref[0] = acc_gu[PAD : PAD + UNITS, :].astype(bf16)
        for half, base in enumerate((core * HALF, HALF - core * HALF)):
            col = pl.ds(pl.multiple_of(base, HALF), HALF)
            gd_ref[0, :, col] = acc_d[:UNITS, half * HALF : (half + 1) * HALF].astype(bf16)


def grads_call(chunk, expert, real, last, core, x_rows, g_parts, act, dgu):
    weight = pl.BlockSpec((1, UNITS, D), lambda i, k, e, r, l, c: (e[i], 0, 0))

    def flat(size, width):
        return pl.BlockSpec((1, size, width), lambda i, k, e, r, l, c: (k[i], 0, 0))

    halves = [flat(size, HALF) for size in SPLIT for _ in range(2)]
    return pl.pallas_call(
        grads_kernel,
        grid_spec=pltpu.PrefetchScalarGridSpec(
            num_scalar_prefetch=5,
            grid=(STEPS,),
            in_specs=[
                pl.BlockSpec((8, 1, CAP, COLS), lambda i, k, e, r, l, c: (0, k[i], 0, 0)),
                *halves,
                flat(CAP, PAD),
                flat(CAP, 2 * PAD),
            ],
            out_specs=[weight, weight, weight],
            scratch_shapes=[pltpu.VMEM((2 * PAD, D), f32), pltpu.VMEM((PAD, D), f32)],
        ),
        out_shape=[jax.ShapeDtypeStruct((EXP_GROUP, UNITS, D), bf16)] * 3,
        compiler_params=pltpu.CompilerParams(vmem_limit_bytes=56 << 20),
        cost_estimate=pl.CostEstimate(
            flops=2 * 3 * FETCH * CAP * D * PAD, bytes_accessed=45 << 20, transcendentals=0
        ),
        name="weight_grads",
    )(chunk, expert, real, last, core, x_rows, *g_parts, act, dgu)


def grad_order(experts):
    ids = jnp.arange(FETCH, dtype=jnp.int32)
    own = jnp.arange(EXP_GROUP, dtype=jnp.int32)
    listed = experts[None, :] == own[:, None]
    first = jnp.min(jnp.where(listed, ids[None, :], FETCH), axis=1)
    first = jnp.where(first == FETCH, 0, first)
    key = jnp.concatenate([own * 32, experts * 32 + 1 + ids])
    chunk = jnp.concatenate([first, ids])
    owner = jnp.concatenate([own, experts])
    rank = jnp.sum((key[None, :] < key[:, None]).astype(jnp.int32), axis=1)
    place = rank[:, None] == jnp.arange(STEPS, dtype=jnp.int32)[None, :]

    def ordered(values):
        return jnp.sum(jnp.where(place, values[:, None], 0), axis=0)

    count = jnp.sum((owner[None, :] == owner[:, None]) & (key[None, :] > key[:, None]), axis=1)
    earlier = (experts[None, :] == experts[:, None]) & (ids[None, :] < ids[:, None])
    again = jnp.any(earlier, axis=1).astype(jnp.int32)
    real = jnp.concatenate([jnp.zeros((EXP_GROUP,), jnp.int32), 1 + again])
    last = (count == 0).astype(jnp.int32)
    return ordered(chunk), ordered(owner), ordered(real), ordered(last)


def rows_order(experts):
    ids = jnp.arange(FETCH, dtype=jnp.int32)
    key = experts * FETCH + ids
    rank = jnp.sum((key[None, :] < key[:, None]).astype(jnp.int32), axis=1)
    place = rank[:, None] == ids[None, :]
    order = jnp.sum(jnp.where(place, ids[:, None], 0), axis=0)
    expert = jnp.sum(jnp.where(place, experts[:, None], 0), axis=0)
    earlier = (experts[None, :] == experts[:, None]) & (ids[None, :] < ids[:, None])
    new = 1 - jnp.any(earlier, axis=1).astype(jnp.int32)
    fresh = jnp.sum(jnp.where(place, new[:, None], 0), axis=0)
    return order, expert, fresh


Z_GROUPS = [[0, 2, 4, 6], [1, 3, 5, 7]]
PAIRS = [(i, i ^ 1) for i in range(8)]


def after(value, *others):
    return lax.optimization_barrier((value,) + others)[0]


def exchange(value, axis="group"):
    return lax.all_to_all(value, axis, split_axis=0, concat_axis=0, tiled=True)


def swap(value):
    return lax.ppermute(value, "hidden", PAIRS)


def shards(
    queries, key_rows, value_rows, out_proj, residual, norm_gain, w_gate, w_up, w_down,
    route_slot, route_weight, fetch_list, cotangent,
):
    tokens = queries.shape[0]
    hidden = lax.axis_index("hidden")
    group = lax.axis_index("group")
    core = hidden % 2
    core_arr = core.reshape(1).astype(jnp.int32)
    wg, wu = w_gate.transpose(0, 2, 1), w_up.transpose(0, 2, 1)
    weights = [wg, wu, w_down, swap(wg), swap(wu), swap(w_down)]

    kv = hidden * (queries.shape[1] // HEAD_DIM) // (HEADS // KV_HEADS)
    key_block = lax.dynamic_slice_in_dim(key_rows, kv * HEAD_DIM, HEAD_DIM, 1)
    value_block = lax.dynamic_slice_in_dim(value_rows, kv * HEAD_DIM, HEAD_DIM, 1)
    mixed = attention(queries, key_block, value_block)
    proj = out_proj.reshape(out_proj.shape[0], 8, COLS)
    part = jnp.einsum("tk,khc->htc", mixed, proj, preferred_element_type=f32).astype(bf16)
    attn = lax.psum_scatter(part, "hidden", scatter_dimension=0, tiled=True)[0]

    route_slot = after(route_slot, part)
    slot_ids = jnp.arange(FETCH, dtype=jnp.int32)
    chosen = route_slot[:, :, None] == slot_ids[None, None, :]
    slot_weight = jnp.sum(jnp.where(chosen, route_weight[:, :, None], 0.0), axis=1)
    used = jnp.any(chosen, axis=1)
    lower = (
        lax.broadcasted_iota(jnp.int32, (tokens, tokens), 0)
        >= lax.broadcasted_iota(jnp.int32, (tokens, tokens), 1)
    ).astype(bf16)
    position = mm(lower, used.astype(bf16), NN).astype(jnp.int32) - 1
    position = jnp.where(used, position, -1)
    pos_t, weight_t = position.T, slot_weight.T

    def one_hot(start, size):
        caps = start + jnp.arange(size, dtype=jnp.int32)
        hit = pos_t[:, None, :] == caps[None, :, None]
        weight = jnp.sum(jnp.where(hit, weight_t[:, None, :], 0.0), axis=2)
        return hit.astype(bf16).reshape(FETCH * size, tokens), weight.reshape(-1, 1)

    row_slot = lax.broadcasted_iota(jnp.int32, (FETCH, FETCH * CAP), 1) // CAP
    spread = (row_slot == lax.broadcasted_iota(jnp.int32, (FETCH, FETCH * CAP), 0)).astype(bf16)
    row_cap = lax.broadcasted_iota(jnp.int32, (tokens, FETCH * CAP), 1) % CAP
    hit_rows = mm(position.astype(bf16), spread, NN) == row_cap.astype(f32)
    high = slot_weight.astype(bf16)
    low = (slot_weight - high.astype(f32)).astype(bf16)
    into = hit_rows.astype(bf16)
    into_high = jnp.where(hit_rows, mm(high, spread, NN), 0.0).astype(bf16)
    into_low = jnp.where(hit_rows, mm(low, spread, NN), 0.0).astype(bf16)

    cot_half = lax.dynamic_slice_in_dim(cotangent, core * HALF, HALF, 1)

    def grad_rows(start, size):
        pick, weight = one_hot(start, size)
        return (mm(pick, cot_half, NN) * weight).astype(bf16).reshape(FETCH, size, HALF)

    pick, row_weight = one_hot(0, CAP)
    g_first = exchange(after(grad_rows(0, SPLIT[0]), pick, row_weight))

    second_rows = grad_rows(SPLIT[0], SPLIT[1])
    own_col = lax.dynamic_slice_in_dim(fetch_list, group, 1, 1)[:, 0]
    experts = own_col - group * EXP_GROUP
    scalars = (*rows_order(experts), core_arr)
    tables = grad_order(experts)
    attn, second_rows, scalars, tables, into, into_high, into_low, weights = (
        lax.optimization_barrier(
            (attn, second_rows, scalars, tables, into, into_high, into_low, weights)
        )
    )
    first_col = hidden * COLS
    res_share = lax.dynamic_slice_in_dim(residual, first_col, COLS, 1)
    gain = lax.dynamic_slice_in_dim(norm_gain, first_col, COLS, 0)
    stream = res_share.astype(f32) + attn.astype(f32)
    own_square = jnp.sum(stream * stream, axis=1)
    square = own_square
    for turn in range(1, 8):
        square = square + lax.ppermute(own_square, "hidden", [(i, i ^ turn) for i in range(8)])
    square = square / D
    normed = (stream * lax.rsqrt(square + epsilon)[:, None] * gain[None, :]).astype(bf16)

    x_part = mm(pick, normed, NN).astype(bf16).reshape(FETCH, CAP, COLS)
    x_part = exchange(after(x_part, g_first))
    x_rows = lax.all_gather(x_part, "hidden", axis=0, tiled=False)
    g_second = exchange(after(second_rows, x_part))
    g_parts = [g_first, swap(after(g_first, g_second)), g_second, swap(g_second)]

    out_rows, act, dgu, d_half = rows_call(scalars, x_rows, g_parts, weights)

    out_share = lax.psum_scatter(
        out_rows, "hidden", scatter_dimension=0, tiled=True, axis_index_groups=Z_GROUPS
    )[0]
    d_back = exchange(d_half)
    grad_gate, grad_up, grad_down = grads_call(
        *tables, core_arr, x_rows, g_parts, after(act, d_back), dgu
    )
    out_back = exchange(after(out_share, d_back))

    d_tok = mm(into, d_back.reshape(-1, HALF), NN).astype(bf16)
    d_tok = d_tok.reshape(tokens, 4, COLS).transpose(1, 0, 2)
    grad_normed = lax.psum_scatter(
        d_tok, "hidden", scatter_dimension=0, tiled=True, axis_index_groups=Z_GROUPS
    )[0]

    out_back = out_back.reshape(-1, COLS)
    moe = mm(into_high, out_back, NN) + mm(into_low, out_back, NN)
    layer_out = (stream + moe).astype(bf16)
    return (
        layer_out,
        grad_normed,
        grad_gate.transpose(0, 2, 1),
        grad_up.transpose(0, 2, 1),
        grad_down,
    )


def solution(mesh):
    return jax.shard_map(
        shards,
        mesh=mesh,
        in_specs=(
            P("group", "hidden"),
            P("group", None),
            P("group", None),
            P("hidden", None),
            P("group", None),
            P(),
            P("group", None, "hidden"),
            P("group", None, "hidden"),
            P("group", "hidden", None),
            P("group", None),
            P("group", None),
            P(),
            P("group", None),
        ),
        out_specs=(
            P("group", "hidden"),
            P("group", "hidden"),
            P("group", None, "hidden"),
            P("group", None, "hidden"),
            P("group", "hidden", None),
        ),
        check_vma=False,
    )
```
